32 devices in a mesh: tm: 8 (over z, core), zone: 4 (over y, x).
Axes of the slice: x: 2, y: 2, z: 4, core: 2. Of those that a mesh axis runs over, the one named last changes fastest.
Arguments:
- initial_guess: float32 [15, 3, 4, 1024], P(None, None, 'zone', 'tm'), may hold values from -2.5 to 2.5
- harmonic_loads: float32 [15, 3, 4, 1024], P(None, None, 'zone', 'tm'), may hold values from -12 to 12
- stiffness: bfloat16 [4, 8, 5, 384, 384], P('zone', 'tm'), as said below
- mass_tiles: bfloat16 [4, 8, 384, 384], P('zone', 'tm'), as said below
- block_links: int32 [4, 8, 2], P('zone', 'tm'), may hold values from 0 to 7, as said below
- states: int32 [2048, 4, 1024], P('tm', 'zone'), may hold values from 0 to 2
- preload: float32 [4, 1024], P('zone'), may hold values from 1 to 3
- normal_stiff: float32 [4, 1024], P('zone'), may hold values from 0.5 to 2
- tangent_stiff: float32 [4, 1024], P('zone'), may hold values from 0.3 to 1.5
- friction: float32 [4, 1024], P('zone'), may hold values from 0.2 to 0.8
Outputs:
- coefficients: float32 [15, 3, 4, 1024], P(None, None, 'zone', 'tm')
- residual: float32 [15, 3, 4, 1024], P(None, None, 'zone', 'tm')
The draws below stay inside these ranges and needn't reach their ends.
Inputs may be any that keep to these rules, and one draw needn't show every extreme that they name: `block_links`: in each row the 2 entries are distinct and differ from the row's own block index (the second index). `stiffness`: in slot 0 every diagonal entry lies between 4 and 8. `mass_tiles`: every diagonal entry lies between 0.5 and 1.
All inputs are finite; a program needn't handle non-finite values.
Results may differ from the reference program's by a relative error of at most 0.0003.
Values sent between devices are 32-bit elements; how exact they have to be, the bound alone decides.
A program may use at most 64 MiB of HBM per device.

```python
import math
import jax
import jax.numpy as jnp
from jax import lax

COEFFS = 15
SAMPLES = 2048
DIRS = 3
BLOCK = 128
ZONE_NODES = 1024
ZONE_BLOCKS = 8
ZONES = 4
SLOTS = 5
ITERS = 2


OFF_DIAGONAL = 0.8


MASS_SPREAD = 0.2


def diagonal_marker(block_width):
    return (lax.broadcasted_iota(jnp.int32, (block_width, block_width), 0) == lax.broadcasted_iota(jnp.int32, (block_width, block_width), 1)).astype(jnp.float32)


def draw_stiffness(key, part):
    block_width = DIRS * BLOCK
    first_key, second_key = jax.random.split(jax.random.fold_in(key, 11))
    tile_shape = (ZONES, ZONE_BLOCKS, SLOTS, block_width, block_width)
    diag_shape = (ZONES, ZONE_BLOCKS, block_width)
    spread = jnp.clip(jax.random.normal(first_key, tile_shape, jnp.float32), -4.0, 4.0)
    diagonal = jnp.exp(jax.random.uniform(second_key, diag_shape, jnp.float32, math.log(4.0), math.log(8.0)))
    identity = diagonal_marker(block_width)
    first_slot = (jnp.arange(SLOTS) == 0).astype(jnp.float32)
    placed = identity[None, :, :] * first_slot[:, None, None]
    tile_values = spread * (OFF_DIAGONAL / math.sqrt(block_width)) * (1.0 - placed) + placed * diagonal[:, :, None, :, None]
    return tile_values.astype(jnp.bfloat16)


def draw_mass_tiles(key, part):
    block_width = DIRS * BLOCK
    first_key, second_key = jax.random.split(jax.random.fold_in(key, 23))
    tile_shape = (ZONES, ZONE_BLOCKS, block_width, block_width)
    diag_shape = (ZONES, ZONE_BLOCKS, block_width)
    spread = jnp.clip(jax.random.normal(first_key, tile_shape, jnp.float32), -4.0, 4.0)
    diagonal = jnp.exp(jax.random.uniform(second_key, diag_shape, jnp.float32, math.log(0.5), 0.0))
    identity = diagonal_marker(block_width)
    tile_values = spread * (MASS_SPREAD / math.sqrt(block_width)) * (1.0 - identity) + identity * diagonal[:, :, :, None]
    return tile_values.astype(jnp.bfloat16)


def draw_block_links(key, part):
    first_key, second_key = jax.random.split(jax.random.fold_in(key, 37))
    row_shape = (ZONES, ZONE_BLOCKS)
    first_offset = jax.random.randint(first_key, row_shape, 1, ZONE_BLOCKS)
    extra_step = jax.random.randint(second_key, row_shape, 1, ZONE_BLOCKS - 1)
    second_offset = 1 + (first_offset - 1 + extra_step) % (ZONE_BLOCKS - 1)
    own_index = lax.broadcasted_iota(jnp.int32, row_shape, 1)
    offsets = jnp.stack([first_offset, second_offset], axis=-1)
    return ((own_index[:, :, None] + offsets) % ZONE_BLOCKS).astype(jnp.int32)


def place_ends(array, own_key, smallest, high):
    longest = array.shape.index(max(array.shape))
    spots = []
    for shift in (0, 1):
        where = [jax.random.randint(jax.random.fold_in(own_key, axis), (), 0, length) for axis, length in enumerate(array.shape)]
        where[longest] = (where[longest] + shift) % array.shape[longest]
        spots.append(tuple(where))
    return array.at[spots[0]].set(smallest).at[spots[1]].set(high)


def block_scale(key, extent, pieces, smallest, high):
    factor_of = 1.0
    for position, parts in pieces:
        draws = jax.random.uniform(jax.random.fold_in(jax.random.fold_in(key, 6), position), (parts,), jnp.float32, smallest / len(pieces), high / len(pieces))
        factor_of = factor_of * jnp.repeat(jnp.exp(draws), extent[position] // parts).reshape((-1,) + (1,) * (len(extent) - 1 - position))
    return factor_of


def centred(stream_key, dims, width, reach, pieces=(), kind=jnp.bfloat16):
    entries = jax.random.normal(stream_key, dims, jnp.float32) * width
    if len(pieces) > 0:
        entries = block_scale(stream_key, dims, pieces, -0.22, 0.18) * entries
    return jnp.clip(entries, min=-reach, max=reach).astype(kind)


def setup_inputs(seed: int = 0) -> dict:
    keys = jax.random.split(jax.random.key(seed), 11)
    return {
        "initial_guess": centred(keys[0], (COEFFS, DIRS, ZONES, ZONE_NODES), 0.3, 2.5, ((2, 4), (3, 8)), jnp.float32),
        "harmonic_loads": centred(keys[1], (COEFFS, DIRS, ZONES, ZONE_NODES), 2.0, 12.0, ((2, 4), (3, 8)), jnp.float32),
        "stiffness": draw_stiffness(jax.random.fold_in(keys[10], 71), 0),
        "mass_tiles": draw_mass_tiles(jax.random.fold_in(keys[10], 71), 0),
        "block_links": draw_block_links(jax.random.fold_in(keys[10], 71), 0),
        "states": place_ends(jax.random.randint(keys[5], (SAMPLES, ZONES, ZONE_NODES), 0, 3), jax.random.fold_in(keys[5], 1), 0, 2).astype(jnp.int32),
        "preload": jnp.clip(1.0 + 2.0 * jax.random.uniform(keys[6], (ZONES, ZONE_NODES), jnp.float32) ** block_scale(keys[6], (ZONES, ZONE_NODES), ((0, 4),), -0.2, 0.2), 1.0, 3.0),
        "normal_stiff": jnp.clip(jnp.exp(math.log(2.0) - 1.3862944 * jax.random.uniform(keys[7], (ZONES, ZONE_NODES), jnp.float32) ** block_scale(keys[7], (ZONES, ZONE_NODES), ((0, 4),), -0.2, 0.2)), 0.5, 2.0),
        "tangent_stiff": jnp.clip(jnp.exp(math.log(1.5) - 1.60943787 * jax.random.uniform(keys[8], (ZONES, ZONE_NODES), jnp.float32) ** block_scale(keys[8], (ZONES, ZONE_NODES), ((0, 4),), -0.2, 0.2)), 0.3, 1.5),
        "friction": jnp.clip(0.2 + 0.6 * jax.random.uniform(keys[9], (ZONES, ZONE_NODES), jnp.float32) ** block_scale(keys[9], (ZONES, ZONE_NODES), ((0, 4),), -0.2, 0.2), 0.2, 0.8),
    }


OMEGA_SQUARED = 0.05
SMOOTHING = 0.1
FULL_PRECISION = lax.Precision.HIGHEST

def harmonic_orders(coeff_count):
    row_index = jnp.arange(coeff_count, dtype=jnp.int32)
    return (row_index + 1) // 2

def synthesis_table(first_sample, sample_count, total_samples, coeff_count):
    samples_here = first_sample + jnp.arange(sample_count, dtype=jnp.int32)
    orders = harmonic_orders(coeff_count)
    phases = samples_here[:, None] * orders[None, :] % total_samples
    angles = phases.astype(jnp.float32) * (2.0 * math.pi / total_samples)
    row_index = jnp.arange(coeff_count, dtype=jnp.int32)
    is_sine = (row_index % 2 == 0) & (row_index > 0)
    return jnp.where(is_sine[None, :], jnp.sin(angles), jnp.cos(angles))

def analysis_table(synthesis, coeff_count, total_samples):
    orders = harmonic_orders(coeff_count)
    scaling = jnp.where(orders == 0, 1.0, 2.0) / total_samples
    return synthesis * scaling[None, :]

def contact_law(motion, states, preload, normal_stiff, tangent_stiff, friction):
    normal_part = preload + normal_stiff * motion[:, 0]
    slide_one = motion[:, 1]
    slide_two = motion[:, 2]
    magnitude = jnp.sqrt(slide_one * slide_one + slide_two * slide_two + SMOOTHING * SMOOTHING)
    touching = states > 0
    sticking = states == 1
    normal_force = jnp.where(touching, normal_part, 0.0)
    slip_factor = friction * normal_force / magnitude
    tangent_factor = jnp.where(sticking, tangent_stiff, slip_factor)
    tangent_factor = jnp.where(touching, tangent_factor, 0.0)
    return jnp.stack([normal_force, tangent_factor * slide_one, tangent_factor * slide_two], axis=1)

def block_view(coeff_field):
    coeff_count, direction_count, node_count = coeff_field.shape
    divided = coeff_field.reshape(coeff_count, direction_count, node_count // BLOCK, BLOCK)
    return divided.transpose(2, 0, 1, 3).reshape(node_count // BLOCK, coeff_count, direction_count * BLOCK)

def field_view(blocks):
    block_count, coeff_count, block_width = blocks.shape
    divided = blocks.reshape(block_count, coeff_count, DIRS, BLOCK)
    return divided.transpose(1, 2, 0, 3).reshape(coeff_count, DIRS, block_count * BLOCK)

def coupled_update(own_field, zone_coeffs, sectors, stiffness, mass_tiles, block_links, forces, own_loads):
    orders = harmonic_orders(own_field.shape[0]).astype(jnp.float32)
    inertia = OMEGA_SQUARED * orders * orders
    own_blocks = block_view(own_field)
    zone_blocks = block_view(zone_coeffs)
    before_blocks = block_view(sectors[:, :, 0, :])
    after_blocks = block_view(sectors[:, :, 2, :])
    linked = zone_blocks[block_links]
    sources = jnp.concatenate([own_blocks[:, None], before_blocks[:, None], after_blocks[:, None], linked], axis=1)
    elastic = jnp.einsum('bshi,bsij->bhj', sources, stiffness.astype(jnp.float32), precision=FULL_PRECISION)
    kinetic = jnp.einsum('bhi,bij->bhj', own_blocks, mass_tiles.astype(jnp.float32), precision=FULL_PRECISION)
    coupled = elastic - inertia[None, :, None] * kinetic
    residual = field_view(coupled) + forces - own_loads
    stiff_diag = jnp.diagonal(stiffness[:, 0].astype(jnp.float32), axis1=-2, axis2=-1)
    mass_diag = jnp.diagonal(mass_tiles.astype(jnp.float32), axis1=-2, axis2=-1)
    pivots = stiff_diag[:, None, :] - inertia[None, :, None] * mass_diag[:, None, :]
    return (residual, own_field - residual / field_view(pivots))

def zone_forces(inputs):
    zone_coeffs, zone_states, preload, normal_stiff, tangent_stiff, friction = inputs
    synthesis = synthesis_table(0, SAMPLES, SAMPLES, COEFFS)
    analysis = analysis_table(synthesis, COEFFS, SAMPLES)
    motion = jnp.einsum('th,hdn->tdn', synthesis, zone_coeffs, precision=FULL_PRECISION)
    forces_time = contact_law(motion, zone_states, preload, normal_stiff, tangent_stiff, friction)
    return jnp.einsum('th,tdn->hdn', analysis, forces_time, precision=FULL_PRECISION)

def zone_update(inputs):
    own_field, before_zone, after_zone, stiffness, mass_tiles, block_links, forces, own_loads = inputs
    sectors = jnp.stack([before_zone, own_field, after_zone], axis=2)
    return coupled_update(own_field, own_field, sectors, stiffness, mass_tiles, block_links, forces, own_loads)

def reference(initial_guess, harmonic_loads, stiffness, mass_tiles, block_links, states, preload, normal_stiff, tangent_stiff, friction):
    zone_major = initial_guess.transpose(2, 0, 1, 3)
    loads_major = harmonic_loads.transpose(2, 0, 1, 3)
    state_major = states.transpose(1, 0, 2)
    residual = zone_major
    for iteration in range(ITERS):
        forces = lax.map(zone_forces, (zone_major, state_major, preload, normal_stiff, tangent_stiff, friction))
        before_zone = jnp.roll(zone_major, 1, axis=0)
        after_zone = jnp.roll(zone_major, -1, axis=0)
        residual, zone_major = lax.map(zone_update, (zone_major, before_zone, after_zone, stiffness, mass_tiles, block_links, forces, loads_major))
    return (zone_major.transpose(1, 2, 0, 3), residual.transpose(1, 2, 0, 3))
```

```python
import functools
import math

import jax
import jax.numpy as jnp
import ml_dtypes
import numpy as np
from jax import lax
from jax.experimental import pallas as pl
from jax.experimental.pallas import tpu as pltpu
from jax.sharding import PartitionSpec as P

DIRS = 3
BLOCK = 128
ITERS = 2
ROWS = 16
WIDTH = DIRS * BLOCK
OMEGA_SQUARED = 0.05
SMOOTHING = 0.1
MESH = pl.DeviceIdType.MESH


def split_np(table):
    high = table.astype(ml_dtypes.bfloat16)
    low = (table - high.astype(np.float64)).astype(ml_dtypes.bfloat16)
    return high, low


def trig_tables(total_samples, coeff_count, parts):
    rows = np.arange(coeff_count)
    orders = (rows + 1) // 2
    phases = (np.arange(total_samples)[:, None] * orders[None, :]) % total_samples
    angles = phases * (2.0 * math.pi / total_samples)
    is_sine = (rows % 2 == 0) & (rows > 0)
    synthesis = np.zeros((total_samples, ROWS))
    synthesis[:, :coeff_count] = np.where(is_sine[None, :], np.sin(angles), np.cos(angles))
    scaling = np.zeros(ROWS)
    scaling[:coeff_count] = np.where(orders == 0, 1.0, 2.0) / total_samples
    analysis = synthesis * scaling[None, :]
    s_high, s_low = split_np(synthesis)
    a_high, a_low = split_np(analysis)
    samples = total_samples // parts
    stacked = np.concatenate([s_high, s_high, s_low], axis=1).reshape(parts, samples, 3 * ROWS)
    stacked_t = np.concatenate([a_high, a_low], axis=1).reshape(parts, samples, 2 * ROWS)
    return stacked, np.ascontiguousarray(stacked_t.transpose(0, 2, 1))


def split(values):
    high = values.astype(jnp.bfloat16)
    low = (values - high.astype(jnp.float32)).astype(jnp.bfloat16)
    return high, low


def mm(a, b):
    return jnp.dot(a, b, preferred_element_type=jnp.float32)


def xor_index(index, k):
    result = index
    bit = 1
    while bit <= k:
        if k & bit:
            result = result + bit * (1 - 2 * ((index // bit) % 2))
        bit *= 2
    return result


def kernel(
    n,
    zones,
    coeff_count,
    guess,
    loads,
    stiff_hbm,
    mass_hbm,
    links,
    states_hbm,
    preload,
    normal_stiff,
    tangent_stiff,
    friction,
    syn_hbm,
    ana_hbm,
    out_coeff,
    out_res,
    xin,
    lin,
    stiff,
    mass,
    states,
    syn,
    ana,
    field,
    load_field,
    zone_first,
    zone_second,
    near_x,
    part,
    recv,
    local_sem,
    state_sem,
    ag_send,
    ag_recv,
    near_send,
    near_recv,
    rs_send,
    rs_recv,
):
    me = lax.axis_index("tm")
    zone = lax.axis_index("zone")
    before = lax.rem(zone + zones - 1, zones)
    after = lax.rem(zone + 1, zones)
    peers = [xor_index(me, k) for k in range(n)]

    fetch_x = [
        pltpu.make_async_copy(guess.at[:, d, 0, :], xin.at[d], local_sem.at[d]) for d in range(DIRS)
    ]
    fetch_tables = [
        pltpu.make_async_copy(syn_hbm.at[me], syn, local_sem.at[3]),
        pltpu.make_async_copy(ana_hbm.at[me], ana, local_sem.at[4]),
    ]
    fetch_states = [
        pltpu.make_async_copy(states_hbm.at[:, peers[k], :], states.at[k], state_sem.at[k])
        for k in range(n)
    ]
    fetch_tiles = [
        pltpu.make_async_copy(stiff_hbm.at[0, 0], stiff, local_sem.at[5]),
        pltpu.make_async_copy(mass_hbm.at[0, 0], mass, local_sem.at[6]),
    ]
    fetch_loads = [
        pltpu.make_async_copy(loads.at[:, d, 0, :], lin.at[d], local_sem.at[7 + d])
        for d in range(DIRS)
    ]
    for copy in fetch_x + fetch_tables + fetch_states[:1] + fetch_tiles + fetch_states[1:] + fetch_loads:
        copy.start()

    barrier = pltpu.get_barrier_semaphore()
    for k in range(1, n):
        pl.semaphore_signal(barrier, inc=1, device_id=(peers[k], zone), device_id_type=MESH)
    for other in (before, after):
        pl.semaphore_signal(barrier, inc=1, device_id=(me, other), device_id_type=MESH)

    field[...] = jnp.zeros_like(field)
    load_field[...] = jnp.zeros_like(load_field)
    for copy in fetch_x:
        copy.wait()
    for d in range(DIRS):
        field[:coeff_count, d * BLOCK : (d + 1) * BLOCK] = xin[d]
    pl.semaphore_wait(barrier, n + 1)

    row_id = lax.broadcasted_iota(jnp.int32, (ROWS, WIDTH), 0)
    order = ((row_id + 1) // 2).astype(jnp.float32)
    inertia = OMEGA_SQUARED * order * order
    constant_row = (lax.broadcasted_iota(jnp.int32, (ROWS, BLOCK), 0) == 0).astype(jnp.float32)

    def partial_forces(x, k):
        b = pl.ds(peers[k], 1)
        normal_x = x[:, :BLOCK] * normal_stiff[b, :] + constant_row * preload[b, :]
        high, low = split(jnp.concatenate([normal_x, x[:, BLOCK:]], axis=1))
        motion = mm(syn[...], jnp.concatenate([high, low, high], axis=0))
        state = states[k]
        u1 = motion[:, BLOCK : 2 * BLOCK]
        u2 = motion[:, 2 * BLOCK :]
        inverse = lax.rsqrt(u1 * u1 + u2 * u2 + SMOOTHING * SMOOTHING)
        normal = jnp.where(state > 0, motion[:, :BLOCK], 0.0)
        factor = jnp.where(state == 1, tangent_stiff[b, :], friction[b, :] * normal * inverse)
        f_high, f_low = split(jnp.concatenate([normal, factor * u1, factor * u2], axis=1))
        first = mm(ana[...], f_high)
        return first[:ROWS] + first[ROWS:] + mm(ana[:ROWS, :], f_low)

    def both(x):
        return jnp.concatenate(split(x), axis=0)

    sent = []
    residual = None
    pivots = None
    far_first = list(range(n - 1, 0, -1))
    for it in range(ITERS):
        x = field[...]
        zone_x = (zone_first, zone_second)[it]
        zone_x[me] = x
        gather = {}
        for k in far_first:
            gather[k] = pltpu.make_async_remote_copy(
                src_ref=zone_x.at[me],
                dst_ref=zone_x.at[me],
                send_sem=ag_send.at[it, k],
                recv_sem=ag_recv.at[it, k],
                device_id=(peers[k], zone),
                device_id_type=MESH,
            )
            gather[k].start()
        near = []
        for side, other in enumerate((after, before)):
            copy = pltpu.make_async_remote_copy(
                src_ref=zone_x.at[me],
                dst_ref=near_x.at[it, side],
                send_sem=near_send.at[it, side],
                recv_sem=near_recv.at[it, side],
                device_id=(me, other),
                device_id_type=MESH,
            )
            copy.start()
            near.append(copy)
        if it == 0:
            for copy in fetch_tables:
                copy.wait()
            fetch_states[0].wait()
        total = partial_forces(x, 0)
        if it == 0:
            for copy in fetch_tiles + fetch_loads:
                copy.wait()
            for d in range(DIRS):
                load_field[:coeff_count, d * BLOCK : (d + 1) * BLOCK] = lin[d]
            eye = lax.broadcasted_iota(jnp.int32, (BLOCK, BLOCK), 0) == lax.broadcasted_iota(
                jnp.int32, (BLOCK, BLOCK), 1
            )

            def diagonal(load):
                return jnp.concatenate(
                    [
                        jnp.sum(
                            jnp.where(eye, load(d).astype(jnp.float32), 0.0),
                            axis=0,
                            keepdims=True,
                        )
                        for d in range(DIRS)
                    ],
                    axis=1,
                )

            def tile(d):
                return pl.ds(d * BLOCK, BLOCK)

            pivots = diagonal(lambda d: stiff[0, tile(d), tile(d)]) - inertia * diagonal(
                lambda d: mass[tile(d), tile(d)]
            )
        coupled = mm(both(x), stiff[0]) + mm(both(-inertia * x), mass[...])
        scatter = []
        for k in range(1, n):
            gather[k].wait_recv()
            if it == 0:
                fetch_states[k].wait()
            part[it, k] = partial_forces(zone_x[peers[k]], k)
            copy = pltpu.make_async_remote_copy(
                src_ref=part.at[it, k],
                dst_ref=recv.at[it, k],
                send_sem=rs_send.at[it, k],
                recv_sem=rs_recv.at[it, k],
                device_id=(peers[k], zone),
                device_id_type=MESH,
            )
            copy.start()
            scatter.append(copy)
        for side in range(2):
            near[side].wait_recv()
            coupled = coupled + mm(both(near_x[it, side]), stiff[1 + side])
        for slot in range(3, 5):
            coupled = coupled + mm(both(zone_x[links[0, 0, slot - 3]]), stiff[slot])
        total = total + coupled[:ROWS] + coupled[ROWS:] - load_field[...]
        for k, copy in enumerate(scatter):
            copy.wait_recv()
            total = total + recv[it, k + 1]
        residual = total
        field[...] = x - residual / pivots
        sent += list(gather.values()) + near + scatter

    stores = []
    for d in range(DIRS):
        lanes = pl.ds(d * BLOCK, BLOCK)
        xin[d] = field[:coeff_count, lanes]
        lin[d] = residual[:coeff_count, d * BLOCK : (d + 1) * BLOCK]
        stores.append(
            pltpu.make_async_copy(xin.at[d], out_coeff.at[:, d, 0, :], local_sem.at[d])
        )
        stores.append(
            pltpu.make_async_copy(lin.at[d], out_res.at[:, d, 0, :], local_sem.at[7 + d])
        )
    for copy in stores:
        copy.start()
    for copy in sent:
        copy.wait_send()
    for copy in stores:
        copy.wait()


def solution(mesh):
    n = mesh.shape["tm"]
    zones = mesh.shape["zone"]

    def per_device(
        initial_guess,
        harmonic_loads,
        stiffness,
        mass_tiles,
        block_links,
        states,
        preload,
        normal_stiff,
        tangent_stiff,
        friction,
    ):
        coeff_count = initial_guess.shape[0]
        samples = states.shape[0]
        slots = stiffness.shape[2]
        syn, ana = trig_tables(samples * n, coeff_count, n)
        hbm = pl.BlockSpec(memory_space=pltpu.HBM)
        vmem = pl.BlockSpec(memory_space=pltpu.VMEM)
        smem = pl.BlockSpec(memory_space=pltpu.SMEM)
        f32, bf16 = jnp.float32, jnp.bfloat16
        dma = pltpu.SemaphoreType.DMA
        out = jax.ShapeDtypeStruct(initial_guess.shape, f32)
        flat = [a.reshape(n, BLOCK) for a in (preload, normal_stiff, tangent_stiff, friction)]
        return pl.pallas_call(
            functools.partial(kernel, n, zones, coeff_count),
            out_shape=(out, out),
            in_specs=[hbm, hbm, hbm, hbm, smem, hbm, vmem, vmem, vmem, vmem, hbm, hbm],
            out_specs=(hbm, hbm),
            scratch_shapes=[
                pltpu.VMEM((DIRS, coeff_count, BLOCK), f32),
                pltpu.VMEM((DIRS, coeff_count, BLOCK), f32),
                pltpu.VMEM((slots, WIDTH, WIDTH), bf16),
                pltpu.VMEM((WIDTH, WIDTH), bf16),
                pltpu.VMEM((n, samples, BLOCK), jnp.int32),
                pltpu.VMEM((samples, 3 * ROWS), bf16),
                pltpu.VMEM((2 * ROWS, samples), bf16),
                pltpu.VMEM((ROWS, WIDTH), f32),
                pltpu.VMEM((ROWS, WIDTH), f32),
                pltpu.VMEM((n, ROWS, WIDTH), f32),
                pltpu.VMEM((n, ROWS, WIDTH), f32),
                pltpu.VMEM((ITERS, 2, ROWS, WIDTH), f32),
                pltpu.VMEM((ITERS, n, ROWS, WIDTH), f32),
                pltpu.VMEM((ITERS, n, ROWS, WIDTH), f32),
                dma((7 + DIRS,)),
                dma((n,)),
                dma((ITERS, n)),
                dma((ITERS, n)),
                dma((ITERS, 2)),
                dma((ITERS, 2)),
                dma((ITERS, n)),
                dma((ITERS, n)),
            ],
            compiler_params=pltpu.CompilerParams(
                collective_id=0, has_side_effects=True, vmem_limit_bytes=40 * 1024 * 1024
            ),
        )(
            initial_guess,
            harmonic_loads,
            stiffness,
            mass_tiles,
            block_links,
            states.reshape(samples, n, BLOCK),
            *flat,
            jnp.asarray(syn),
            jnp.asarray(ana),
        )

    return jax.shard_map(
        per_device,
        mesh=mesh,
        in_specs=(
            P(None, None, "zone", "tm"),
            P(None, None, "zone", "tm"),
            P("zone", "tm", None, None, None),
            P("zone", "tm", None, None),
            P("zone", "tm", None),
            P("tm", "zone", None),
            P("zone", None),
            P("zone", None),
            P("zone", None),
            P("zone", None),
        ),
        out_specs=(P(None, None, "zone", "tm"), P(None, None, "zone", "tm")),
        check_vma=False,
    )
```

```python
import functools
import math

import jax
import jax.numpy as jnp
import ml_dtypes
import numpy as np
from jax import lax
from jax.experimental import pallas as pl
from jax.experimental.pallas import tpu as pltpu
from jax.sharding import PartitionSpec as P

DIRS = 3
BLOCK = 128
ITERS = 2
ROWS = 16
WIDTH = DIRS * BLOCK
OMEGA_SQUARED = 0.05
SMOOTHING = 0.1
MESH = pl.DeviceIdType.MESH


def split_np(table):
    high = table.astype(ml_dtypes.bfloat16)
    low = (table - high.astype(np.float64)).astype(ml_dtypes.bfloat16)
    return high, low


def trig_tables(total_samples, coeff_count, parts):
    rows = np.arange(coeff_count)
    orders = (rows + 1) // 2
    phases = (np.arange(total_samples)[:, None] * orders[None, :]) % total_samples
    angles = phases * (2.0 * math.pi / total_samples)
    is_sine = (rows % 2 == 0) & (rows > 0)
    synthesis = np.zeros((total_samples, ROWS))
    synthesis[:, :coeff_count] = np.where(is_sine[None, :], np.sin(angles), np.cos(angles))
    scaling = np.zeros(ROWS)
    scaling[:coeff_count] = np.where(orders == 0, 1.0, 2.0) / total_samples
    analysis = synthesis * scaling[None, :]
    s_high, s_low = split_np(synthesis)
    a_high, a_low = split_np(analysis)
    samples = total_samples // parts
    stacked = np.concatenate([s_high, s_high, s_low], axis=1).reshape(parts, samples, 3 * ROWS)
    stacked_t = np.concatenate([a_high, a_low], axis=1).reshape(parts, samples, 2 * ROWS)
    return stacked, np.ascontiguousarray(stacked_t.transpose(0, 2, 1))


def split(values):
    high = values.astype(jnp.bfloat16)
    low = (values - high.astype(jnp.float32)).astype(jnp.bfloat16)
    return high, low


def mm(a, b):
    return jnp.dot(a, b, preferred_element_type=jnp.float32)


def xor_index(index, k):
    result = index
    bit = 1
    while bit <= k:
        if k & bit:
            result = result + bit * (1 - 2 * ((index // bit) % 2))
        bit *= 2
    return result


def kernel(
    n,
    zones,
    coeff_count,
    guess,
    loads,
    stiff_hbm,
    mass_hbm,
    links,
    states_hbm,
    preload,
    normal_stiff,
    tangent_stiff,
    friction,
    syn_hbm,
    ana_hbm,
    out_coeff,
    out_res,
    xin,
    lin,
    stiff,
    mass,
    states,
    syn,
    ana,
    field,
    load_field,
    zone_first,
    zone_second,
    near_x,
    part,
    recv,
    local_sem,
    state_sem,
    ag_send,
    ag_recv,
    near_send,
    near_recv,
    rs_send,
    rs_recv,
):
    me = lax.axis_index("tm")
    zone = lax.axis_index("zone")
    before = lax.rem(zone + zones - 1, zones)
    after = lax.rem(zone + 1, zones)
    peers = [xor_index(me, k) for k in range(n)]

    fetch_x = [
        pltpu.make_async_copy(guess.at[:, d, 0, :], xin.at[d], local_sem.at[d]) for d in range(DIRS)
    ]
    fetch_tables = [
        pltpu.make_async_copy(syn_hbm.at[me], syn, local_sem.at[3]),
        pltpu.make_async_copy(ana_hbm.at[me], ana, local_sem.at[4]),
    ]
    fetch_states = [
        pltpu.make_async_copy(states_hbm.at[:, peers[k], :], states.at[k], state_sem.at[k])
        for k in range(n)
    ]
    fetch_tiles = [
        pltpu.make_async_copy(stiff_hbm.at[0, 0], stiff, local_sem.at[5]),
        pltpu.make_async_copy(mass_hbm.at[0, 0], mass, local_sem.at[6]),
    ]
    fetch_loads = [
        pltpu.make_async_copy(loads.at[:, d, 0, :], lin.at[d], local_sem.at[7 + d])
        for d in range(DIRS)
    ]
    for copy in fetch_x + fetch_tables + fetch_states[:1] + fetch_tiles + fetch_states[1:] + fetch_loads:
        copy.start()

    barrier = pltpu.get_barrier_semaphore()
    for k in range(1, n):
        pl.semaphore_signal(barrier, inc=1, device_id=(peers[k], zone), device_id_type=MESH)
    for other in (before, after):
        pl.semaphore_signal(barrier, inc=1, device_id=(me, other), device_id_type=MESH)

    field[...] = jnp.zeros_like(field)
    load_field[...] = jnp.zeros_like(load_field)
    for copy in fetch_x:
        copy.wait()
    for d in range(DIRS):
        field[:coeff_count, d * BLOCK : (d + 1) * BLOCK] = xin[d]
    pl.semaphore_wait(barrier, n + 1)

    row_id = lax.broadcasted_iota(jnp.int32, (ROWS, WIDTH), 0)
    order = ((row_id + 1) // 2).astype(jnp.float32)
    inertia = OMEGA_SQUARED * order * order
    constant_row = (lax.broadcasted_iota(jnp.int32, (ROWS, BLOCK), 0) == 0).astype(jnp.float32)

    def partial_forces(x, k):
        b = pl.ds(peers[k], 1)
        normal_x = x[:, :BLOCK] * normal_stiff[b, :] + constant_row * preload[b, :]
        high, low = split(jnp.concatenate([normal_x, x[:, BLOCK:]], axis=1))
        motion = mm(syn[...], jnp.concatenate([high, low, high], axis=0))
        state = states[k]
        u1 = motion[:, BLOCK : 2 * BLOCK]
        u2 = motion[:, 2 * BLOCK :]
        inverse = lax.rsqrt(u1 * u1 + u2 * u2 + SMOOTHING * SMOOTHING)
        normal = jnp.where(state > 0, motion[:, :BLOCK], 0.0)
        factor = jnp.where(state == 1, tangent_stiff[b, :], friction[b, :] * normal * inverse)
        f_high, f_low = split(jnp.concatenate([normal, factor * u1, factor * u2], axis=1))
        first = mm(ana[...], f_high)
        return first[:ROWS] + first[ROWS:] + mm(ana[:ROWS, :], f_low)

    def both(x):
        return jnp.concatenate(split(x), axis=0)

    sent = []
    residual = None
    pivots = None
    far_first = list(range(n - 1, 0, -1))
    for it in range(ITERS):
        x = field[...]
        zone_x = (zone_first, zone_second)[it]
        zone_x[me] = x
        gather = {}
        for k in far_first:
            gather[k] = pltpu.make_async_remote_copy(
                src_ref=zone_x.at[me],
                dst_ref=zone_x.at[me],
                send_sem=ag_send.at[it, k],
                recv_sem=ag_recv.at[it, k],
                device_id=(peers[k], zone),
                device_id_type=MESH,
            )
            gather[k].start()
        near = []
        for side, other in enumerate((after, before)):
            copy = pltpu.make_async_remote_copy(
                src_ref=zone_x.at[me],
                dst_ref=near_x.at[it, side],
                send_sem=near_send.at[it, side],
                recv_sem=near_recv.at[it, side],
                device_id=(me, other),
                device_id_type=MESH,
            )
            copy.start()
            near.append(copy)
        if it == 0:
            for copy in fetch_tables:
                copy.wait()
            fetch_states[0].wait()
        total = partial_forces(x, 0)
        if it == 0:
            for copy in fetch_tiles + fetch_loads:
                copy.wait()
            for d in range(DIRS):
                load_field[:coeff_count, d * BLOCK : (d + 1) * BLOCK] = lin[d]
            eye = lax.broadcasted_iota(jnp.int32, (BLOCK, BLOCK), 0) == lax.broadcasted_iota(
                jnp.int32, (BLOCK, BLOCK), 1
            )

            def diagonal(load):
                return jnp.concatenate(
                    [
                        jnp.sum(
                            jnp.where(eye, load(d).astype(jnp.float32), 0.0),
                            axis=0,
                            keepdims=True,
                        )
                        for d in range(DIRS)
                    ],
                    axis=1,
                )

            def tile(d):
                return pl.ds(d * BLOCK, BLOCK)

            pivots = diagonal(lambda d: stiff[0, tile(d), tile(d)]) - inertia * diagonal(
                lambda d: mass[tile(d), tile(d)]
            )
        coupled = mm(both(x), stiff[0]) + mm(both(-inertia * x), mass[...])
        scatter = []
        for k in range(1, n):
            gather[k].wait_recv()
            if it == 0:
                fetch_states[k].wait()
            part[it, k] = partial_forces(zone_x[peers[k]], k)
            copy = pltpu.make_async_remote_copy(
                src_ref=part.at[it, k],
                dst_ref=recv.at[it, k],
                send_sem=rs_send.at[it, k],
                recv_sem=rs_recv.at[it, k],
                device_id=(peers[k], zone),
                device_id_type=MESH,
            )
            copy.start()
            scatter.append(copy)
        for side in range(2):
            near[side].wait_recv()
            coupled = coupled + mm(both(near_x[it, side]), stiff[1 + side])
        for slot in range(3, 5):
            coupled = coupled + mm(both(zone_x[links[0, 0, slot - 3]]), stiff[slot])
        total = total + coupled[:ROWS] + coupled[ROWS:] - load_field[...]
        for k, copy in enumerate(scatter):
            copy.wait_recv()
            total = total + recv[it, k + 1]
        residual = total
        field[...] = x - residual / pivots
        sent += list(gather.values()) + near + scatter

    stores = []
    for d in range(DIRS):
        lanes = pl.ds(d * BLOCK, BLOCK)
        xin[d] = field[:coeff_count, lanes]
        lin[d] = residual[:coeff_count, d * BLOCK : (d + 1) * BLOCK]
        stores.append(
            pltpu.make_async_copy(xin.at[d], out_coeff.at[:, d, 0, :], local_sem.at[d])
        )
        stores.append(
            pltpu.make_async_copy(lin.at[d], out_res.at[:, d, 0, :], local_sem.at[7 + d])
        )
    for copy in stores:
        copy.start()
    for copy in sent:
        copy.wait_send()
    for copy in stores:
        copy.wait()


def solution(mesh):
    n = mesh.shape["tm"]
    zones = mesh.shape["zone"]

    def per_device(
        initial_guess,
        harmonic_loads,
        stiffness,
        mass_tiles,
        block_links,
        states,
        preload,
        normal_stiff,
        tangent_stiff,
        friction,
    ):
        coeff_count = initial_guess.shape[0]
        samples = states.shape[0]
        slots = stiffness.shape[2]
        syn, ana = trig_tables(samples * n, coeff_count, n)
        hbm = pl.BlockSpec(memory_space=pltpu.HBM)
        vmem = pl.BlockSpec(memory_space=pltpu.VMEM)
        smem = pl.BlockSpec(memory_space=pltpu.SMEM)
        f32, bf16 = jnp.float32, jnp.bfloat16
        dma = pltpu.SemaphoreType.DMA
        out = jax.ShapeDtypeStruct(initial_guess.shape, f32)
        flat = [a.reshape(n, BLOCK) for a in (preload, normal_stiff, tangent_stiff, friction)]
        return pl.pallas_call(
            functools.partial(kernel, n, zones, coeff_count),
            out_shape=(out, out),
            in_specs=[hbm, hbm, hbm, hbm, smem, hbm, vmem, vmem, vmem, vmem, hbm, hbm],
            out_specs=(hbm, hbm),
            scratch_shapes=[
                pltpu.VMEM((DIRS, coeff_count, BLOCK), f32),
                pltpu.VMEM((DIRS, coeff_count, BLOCK), f32),
                pltpu.VMEM((slots, WIDTH, WIDTH), bf16),
                pltpu.VMEM((WIDTH, WIDTH), bf16),
                pltpu.VMEM((n, samples, BLOCK), jnp.int32),
                pltpu.VMEM((samples, 3 * ROWS), bf16),
                pltpu.VMEM((2 * ROWS, samples), bf16),
                pltpu.VMEM((ROWS, WIDTH), f32),
                pltpu.VMEM((ROWS, WIDTH), f32),
                pltpu.VMEM((n, ROWS, WIDTH), f32),
                pltpu.VMEM((n, ROWS, WIDTH), f32),
                pltpu.VMEM((ITERS, 2, ROWS, WIDTH), f32),
                pltpu.VMEM((ITERS, n, ROWS, WIDTH), f32),
                pltpu.VMEM((ITERS, n, ROWS, WIDTH), f32),
                dma((7 + DIRS,)),
                dma((n,)),
                dma((ITERS, n)),
                dma((ITERS, n)),
                dma((ITERS, 2)),
                dma((ITERS, 2)),
                dma((ITERS, n)),
                dma((ITERS, n)),
            ],
            compiler_params=pltpu.CompilerParams(
                collective_id=0, has_side_effects=True, vmem_limit_bytes=60 * 1024 * 1024
            ),
        )(
            initial_guess,
            harmonic_loads,
            stiffness,
            mass_tiles,
            block_links,
            states.reshape(samples, n, BLOCK),
            *flat,
            jnp.asarray(syn),
            jnp.asarray(ana),
        )

    return jax.shard_map(
        per_device,
        mesh=mesh,
        in_specs=(
            P(None, None, "zone", "tm"),
            P(None, None, "zone", "tm"),
            P("zone", "tm", None, None, None),
            P("zone", "tm", None, None),
            P("zone", "tm", None),
            P("tm", "zone", None),
            P("zone", None),
            P("zone", None),
            P("zone", None),
            P("zone", None),
        ),
        out_specs=(P(None, None, "zone", "tm"), P(None, None, "zone", "tm")),
        check_vma=False,
    )
```

```python
import functools
import math

import jax
import jax.numpy as jnp
import ml_dtypes
import numpy as np
from jax import lax
from jax.experimental import pallas as pl
from jax.experimental.pallas import tpu as pltpu
from jax.sharding import PartitionSpec as P

DIRS = 3
BLOCK = 128
ITERS = 2
ROWS = 16
WIDTH = DIRS * BLOCK
OMEGA_SQUARED = 0.05
SMOOTHING = 0.1
MESH = pl.DeviceIdType.MESH


def split_np(table):
    high = table.astype(ml_dtypes.bfloat16)
    low = (table - high.astype(np.float64)).astype(ml_dtypes.bfloat16)
    return high, low


def trig_tables(total_samples, coeff_count, parts):
    rows = np.arange(coeff_count)
    orders = (rows + 1) // 2
    phases = (np.arange(total_samples)[:, None] * orders[None, :]) % total_samples
    angles = phases * (2.0 * math.pi / total_samples)
    is_sine = (rows % 2 == 0) & (rows > 0)
    synthesis = np.zeros((total_samples, ROWS))
    synthesis[:, :coeff_count] = np.where(is_sine[None, :], np.sin(angles), np.cos(angles))
    scaling = np.zeros(ROWS)
    scaling[:coeff_count] = np.where(orders == 0, 1.0, 2.0) / total_samples
    analysis = synthesis * scaling[None, :]
    s_high, s_low = split_np(synthesis)
    a_high, a_low = split_np(analysis)
    samples = total_samples // parts
    stacked = np.concatenate([s_high, s_high, s_low], axis=1).reshape(parts, samples, 3 * ROWS)
    stacked_t = np.concatenate([a_high, a_low], axis=1).reshape(parts, samples, 2 * ROWS)
    return stacked, np.ascontiguousarray(stacked_t.transpose(0, 2, 1))


def split(values):
    high = values.astype(jnp.bfloat16)
    low = (values - high.astype(jnp.float32)).astype(jnp.bfloat16)
    return high, low


def mm(a, b):
    return jnp.dot(a, b, preferred_element_type=jnp.float32)


def xor_index(index, k):
    result = index
    bit = 1
    while bit <= k:
        if k & bit:
            result = result + bit * (1 - 2 * ((index // bit) % 2))
        bit *= 2
    return result


def kernel(
    n,
    zones,
    coeff_count,
    guess,
    loads,
    stiff_hbm,
    mass_hbm,
    links,
    states_hbm,
    preload,
    normal_stiff,
    tangent_stiff,
    friction,
    syn_hbm,
    ana_hbm,
    out_coeff,
    out_res,
    xin,
    lin,
    stiff,
    mass,
    states,
    syn,
    ana,
    field,
    load_field,
    zone_first,
    zone_second,
    near_x,
    part,
    recv,
    local_sem,
    state_sem,
    ag_send,
    ag_recv,
    near_send,
    near_recv,
    rs_send,
    rs_recv,
    fwd_send,
    fwd_recv,
    st_send,
    st_recv,
):
    me = lax.axis_index("tm")
    zone = lax.axis_index("zone")
    before = lax.rem(zone + zones - 1, zones)
    after = lax.rem(zone + 1, zones)
    chips = n // 2
    chip = me // 2
    core = me % 2
    twin = me + 1 - 2 * core
    peers = [2 * xor_index(chip, k) + core for k in range(chips)]
    twins = [2 * xor_index(chip, k) + 1 - core for k in range(chips)]

    fetch_x = [
        pltpu.make_async_copy(guess.at[:, d, 0, :], xin.at[d], local_sem.at[d]) for d in range(DIRS)
    ]
    fetch_tables = [
        pltpu.make_async_copy(syn_hbm.at[me], syn.at[0], local_sem.at[3]),
        pltpu.make_async_copy(ana_hbm.at[me], ana.at[0], local_sem.at[4]),
        pltpu.make_async_copy(syn_hbm.at[twin], syn.at[1], local_sem.at[7 + DIRS]),
        pltpu.make_async_copy(ana_hbm.at[twin], ana.at[1], local_sem.at[8 + DIRS]),
    ]
    fetch_states = [
        pltpu.make_async_copy(states_hbm.at[:, peers[k], :], states.at[0, k], state_sem.at[k])
        for k in range(chips)
    ]
    fetch_tiles = [
        pltpu.make_async_copy(stiff_hbm.at[0, 0], stiff, local_sem.at[5]),
        pltpu.make_async_copy(mass_hbm.at[0, 0], mass, local_sem.at[6]),
    ]
    fetch_loads = [
        pltpu.make_async_copy(loads.at[:, d, 0, :], lin.at[d], local_sem.at[7 + d])
        for d in range(DIRS)
    ]
    for copy in fetch_x + fetch_tables + fetch_states[:1] + fetch_tiles + fetch_states[1:] + fetch_loads:
        copy.start()

    barrier = pltpu.get_barrier_semaphore()
    for peer in peers[1:] + [twin]:
        pl.semaphore_signal(barrier, inc=1, device_id=(peer, zone), device_id_type=MESH)
    for other in (before, after):
        pl.semaphore_signal(barrier, inc=1, device_id=(me, other), device_id_type=MESH)

    field[...] = jnp.zeros_like(field)
    load_field[...] = jnp.zeros_like(load_field)
    for copy in fetch_x:
        copy.wait()
    for d in range(DIRS):
        field[:coeff_count, d * BLOCK : (d + 1) * BLOCK] = xin[d]
    pl.semaphore_wait(barrier, chips + 2)

    row_id = lax.broadcasted_iota(jnp.int32, (ROWS, WIDTH), 0)
    order = ((row_id + 1) // 2).astype(jnp.float32)
    inertia = OMEGA_SQUARED * order * order
    constant_row = (lax.broadcasted_iota(jnp.int32, (ROWS, BLOCK), 0) == 0).astype(jnp.float32)

    def partial_forces(x, k, half):
        b = pl.ds(peers[k], 1)
        normal_x = x[:, :BLOCK] * normal_stiff[b, :] + constant_row * preload[b, :]
        high, low = split(jnp.concatenate([normal_x, x[:, BLOCK:]], axis=1))
        motion = mm(syn[half], jnp.concatenate([high, low, high], axis=0))
        state = states[half, k]
        u1 = motion[:, BLOCK : 2 * BLOCK]
        u2 = motion[:, 2 * BLOCK :]
        inverse = lax.rsqrt(u1 * u1 + u2 * u2 + SMOOTHING * SMOOTHING)
        normal = jnp.where(state > 0, motion[:, :BLOCK], 0.0)
        factor = jnp.where(state == 1, tangent_stiff[b, :], friction[b, :] * normal * inverse)
        f_high, f_low = split(jnp.concatenate([normal, factor * u1, factor * u2], axis=1))
        first = mm(ana[half], f_high)
        return first[:ROWS] + first[ROWS:] + mm(ana[half, :ROWS, :], f_low)

    def both(x):
        return jnp.concatenate(split(x), axis=0)

    def to_twin(ref, index, it, k):
        copy = pltpu.make_async_remote_copy(
            src_ref=ref.at[index],
            dst_ref=ref.at[index],
            send_sem=fwd_send.at[it, k],
            recv_sem=fwd_recv.at[it, k],
            device_id=(twin, zone),
            device_id_type=MESH,
        )
        copy.start()
        return copy

    sent = []
    residual = None
    pivots = None
    far_first = list(range(chips - 1, 0, -1))
    fetch_twin = []
    for it in range(ITERS):
        x = field[...]
        zone_x = (zone_first, zone_second)[it]
        zone_x[me] = x
        gather = {}
        for k in far_first:
            gather[k] = pltpu.make_async_remote_copy(
                src_ref=zone_x.at[me],
                dst_ref=zone_x.at[me],
                send_sem=ag_send.at[it, k],
                recv_sem=ag_recv.at[it, k],
                device_id=(peers[k], zone),
                device_id_type=MESH,
            )
            gather[k].start()
        forward = [to_twin(zone_x, me, it, 0)]
        near = []
        for side, other in enumerate((after, before)):
            copy = pltpu.make_async_remote_copy(
                src_ref=zone_x.at[me],
                dst_ref=near_x.at[it, side],
                send_sem=near_send.at[it, side],
                recv_sem=near_recv.at[it, side],
                device_id=(me, other),
                device_id_type=MESH,
            )
            copy.start()
            near.append(copy)
        if it == 0:
            for k in range(chips):
                copy = pltpu.make_async_remote_copy(
                    src_ref=states_hbm.at[:, twins[k], :],
                    dst_ref=states.at[1, k],
                    send_sem=st_send.at[k],
                    recv_sem=st_recv.at[k],
                    device_id=(twin, zone),
                    device_id_type=MESH,
                )
                copy.start()
                fetch_twin.append(copy)
            for copy in fetch_tables:
                copy.wait()
            fetch_states[0].wait()
        total = partial_forces(x, 0, 0)
        if it == 0:
            fetch_twin[0].wait_recv()
        total = total + partial_forces(x, 0, 1)
        if it == 0:
            for copy in fetch_tiles + fetch_loads:
                copy.wait()
            for d in range(DIRS):
                load_field[:coeff_count, d * BLOCK : (d + 1) * BLOCK] = lin[d]
            eye = lax.broadcasted_iota(jnp.int32, (BLOCK, BLOCK), 0) == lax.broadcasted_iota(
                jnp.int32, (BLOCK, BLOCK), 1
            )

            def diagonal(load):
                return jnp.concatenate(
                    [
                        jnp.sum(
                            jnp.where(eye, load(d).astype(jnp.float32), 0.0),
                            axis=0,
                            keepdims=True,
                        )
                        for d in range(DIRS)
                    ],
                    axis=1,
                )

            def tile(d):
                return pl.ds(d * BLOCK, BLOCK)

            pivots = diagonal(lambda d: stiff[0, tile(d), tile(d)]) - inertia * diagonal(
                lambda d: mass[tile(d), tile(d)]
            )
        coupled = mm(both(x), stiff[0]) + mm(both(-inertia * x), mass[...])
        scatter = []
        for k in range(1, chips):
            gather[k].wait_recv()
            forward.append(to_twin(zone_x, peers[k], it, k))
            if it == 0:
                fetch_states[k].wait()
                fetch_twin[k].wait_recv()
            arrived = zone_x[peers[k]]
            part[it, k] = partial_forces(arrived, k, 0) + partial_forces(arrived, k, 1)
            copy = pltpu.make_async_remote_copy(
                src_ref=part.at[it, k],
                dst_ref=recv.at[it, k],
                send_sem=rs_send.at[it, k],
                recv_sem=rs_recv.at[it, k],
                device_id=(peers[k], zone),
                device_id_type=MESH,
            )
            copy.start()
            scatter.append(copy)
        for side in range(2):
            near[side].wait_recv()
            coupled = coupled + mm(both(near_x[it, side]), stiff[1 + side])
        for copy in forward:
            copy.wait_recv()
        for slot in range(3, 5):
            coupled = coupled + mm(both(zone_x[links[0, 0, slot - 3]]), stiff[slot])
        total = total + coupled[:ROWS] + coupled[ROWS:] - load_field[...]
        for k, copy in enumerate(scatter):
            copy.wait_recv()
            total = total + recv[it, k + 1]
        residual = total
        field[...] = x - residual / pivots
        sent += list(gather.values()) + near + scatter + forward

    stores = []
    for d in range(DIRS):
        lanes = pl.ds(d * BLOCK, BLOCK)
        xin[d] = field[:coeff_count, lanes]
        lin[d] = residual[:coeff_count, d * BLOCK : (d + 1) * BLOCK]
        stores.append(
            pltpu.make_async_copy(xin.at[d], out_coeff.at[:, d, 0, :], local_sem.at[d])
        )
        stores.append(
            pltpu.make_async_copy(lin.at[d], out_res.at[:, d, 0, :], local_sem.at[7 + d])
        )
    for copy in stores:
        copy.start()
    for copy in sent + fetch_twin:
        copy.wait_send()
    for copy in stores:
        copy.wait()


def solution(mesh):
    n = mesh.shape["tm"]
    zones = mesh.shape["zone"]

    def per_device(
        initial_guess,
        harmonic_loads,
        stiffness,
        mass_tiles,
        block_links,
        states,
        preload,
        normal_stiff,
        tangent_stiff,
        friction,
    ):
        coeff_count = initial_guess.shape[0]
        samples = states.shape[0]
        slots = stiffness.shape[2]
        syn, ana = trig_tables(samples * n, coeff_count, n)
        hbm = pl.BlockSpec(memory_space=pltpu.HBM)
        vmem = pl.BlockSpec(memory_space=pltpu.VMEM)
        smem = pl.BlockSpec(memory_space=pltpu.SMEM)
        f32, bf16 = jnp.float32, jnp.bfloat16
        dma = pltpu.SemaphoreType.DMA
        out = jax.ShapeDtypeStruct(initial_guess.shape, f32)
        flat = [a.reshape(n, BLOCK) for a in (preload, normal_stiff, tangent_stiff, friction)]
        return pl.pallas_call(
            functools.partial(kernel, n, zones, coeff_count),
            out_shape=(out, out),
            in_specs=[hbm, hbm, hbm, hbm, smem, hbm, vmem, vmem, vmem, vmem, hbm, hbm],
            out_specs=(hbm, hbm),
            scratch_shapes=[
                pltpu.VMEM((DIRS, coeff_count, BLOCK), f32),
                pltpu.VMEM((DIRS, coeff_count, BLOCK), f32),
                pltpu.VMEM((slots, WIDTH, WIDTH), bf16),
                pltpu.VMEM((WIDTH, WIDTH), bf16),
                pltpu.VMEM((2, n // 2, samples, BLOCK), jnp.int32),
                pltpu.VMEM((2, samples, 3 * ROWS), bf16),
                pltpu.VMEM((2, 2 * ROWS, samples), bf16),
                pltpu.VMEM((ROWS, WIDTH), f32),
                pltpu.VMEM((ROWS, WIDTH), f32),
                pltpu.VMEM((n, ROWS, WIDTH), f32),
                pltpu.VMEM((n, ROWS, WIDTH), f32),
                pltpu.VMEM((ITERS, 2, ROWS, WIDTH), f32),
                pltpu.VMEM((ITERS, n // 2, ROWS, WIDTH), f32),
                pltpu.VMEM((ITERS, n // 2, ROWS, WIDTH), f32),
                dma((9 + DIRS,)),
                dma((n // 2,)),
                dma((ITERS, n // 2)),
                dma((ITERS, n // 2)),
                dma((ITERS, 2)),
                dma((ITERS, 2)),
                dma((ITERS, n // 2)),
                dma((ITERS, n // 2)),
                dma((ITERS, n // 2)),
                dma((ITERS, n // 2)),
                dma((n // 2,)),
                dma((n // 2,)),
            ],
            compiler_params=pltpu.CompilerParams(
                collective_id=0, has_side_effects=True, vmem_limit_bytes=60 * 1024 * 1024
            ),
        )(
            initial_guess,
            harmonic_loads,
            stiffness,
            mass_tiles,
            block_links,
            states.reshape(samples, n, BLOCK),
            *flat,
            jnp.asarray(syn),
            jnp.asarray(ana),
        )

    return jax.shard_map(
        per_device,
        mesh=mesh,
        in_specs=(
            P(None, None, "zone", "tm"),
            P(None, None, "zone", "tm"),
            P("zone", "tm", None, None, None),
            P("zone", "tm", None, None),
            P("zone", "tm", None),
            P("tm", "zone", None),
            P("zone", None),
            P("zone", None),
            P("zone", None),
            P("zone", None),
        ),
        out_specs=(P(None, None, "zone", "tm"), P(None, None, "zone", "tm")),
        check_vma=False,
    )
```

```python
import functools
import math

import jax
import jax.numpy as jnp
import ml_dtypes
import numpy as np
from jax import lax
from jax.experimental import pallas as pl
from jax.experimental.pallas import tpu as pltpu
from jax.sharding import PartitionSpec as P

DIRS = 3
BLOCK = 128
ITERS = 2
ROWS = 16
WIDTH = DIRS * BLOCK
OMEGA_SQUARED = 0.05
SMOOTHING = 0.1
MESH = pl.DeviceIdType.MESH


def split_np(table):
    high = table.astype(ml_dtypes.bfloat16)
    low = (table - high.astype(np.float64)).astype(ml_dtypes.bfloat16)
    return high, low


def trig_tables(total_samples, coeff_count, parts):
    rows = np.arange(coeff_count)
    orders = (rows + 1) // 2
    phases = (np.arange(total_samples)[:, None] * orders[None, :]) % total_samples
    angles = phases * (2.0 * math.pi / total_samples)
    is_sine = (rows % 2 == 0) & (rows > 0)
    synthesis = np.zeros((total_samples, ROWS))
    synthesis[:, :coeff_count] = np.where(is_sine[None, :], np.sin(angles), np.cos(angles))
    scaling = np.zeros(ROWS)
    scaling[:coeff_count] = np.where(orders == 0, 1.0, 2.0) / total_samples
    analysis = synthesis * scaling[None, :]
    s_high, s_low = split_np(synthesis)
    a_high, a_low = split_np(analysis)
    samples = total_samples // parts
    stacked = np.concatenate([s_high, s_high, s_low], axis=1).reshape(parts, samples, 3 * ROWS)
    stacked_t = np.concatenate([a_high, a_low], axis=1).reshape(parts, samples, 2 * ROWS)
    return stacked, np.ascontiguousarray(stacked_t.transpose(0, 2, 1))


def split(values):
    high = values.astype(jnp.bfloat16)
    low = (values - high.astype(jnp.float32)).astype(jnp.bfloat16)
    return high, low


def mm(a, b):
    return jnp.dot(a, b, preferred_element_type=jnp.float32)


def xor_index(index, k):
    result = index
    bit = 1
    while bit <= k:
        if k & bit:
            result = result + bit * (1 - 2 * ((index // bit) % 2))
        bit *= 2
    return result


def kernel(
    n,
    zones,
    coeff_count,
    guess,
    loads,
    stiff_hbm,
    mass_hbm,
    links_hbm,
    states_hbm,
    preload_hbm,
    normal_hbm,
    tangent_hbm,
    friction_hbm,
    syn_hbm,
    ana_hbm,
    out_coeff,
    out_res,
    xin,
    lin,
    stiff,
    mass,
    states,
    syn,
    ana,
    field,
    load_field,
    zone_first,
    zone_second,
    near_x,
    part,
    recv,
    local_sem,
    state_sem,
    ag_send,
    ag_recv,
    near_send,
    near_recv,
    rs_send,
    rs_recv,
    fwd_send,
    fwd_recv,
    st_send,
    st_recv,
    node_sem,
    links,
    preload,
    normal_stiff,
    tangent_stiff,
    friction,
):
    me = lax.axis_index("tm")
    zone = lax.axis_index("zone")
    before = lax.rem(zone + zones - 1, zones)
    after = lax.rem(zone + 1, zones)
    chips = n // 2
    chip = me // 2
    core = me % 2
    twin = me + 1 - 2 * core
    peers = [2 * xor_index(chip, k) + core for k in range(chips)]
    twins = [2 * xor_index(chip, k) + 1 - core for k in range(chips)]

    fetch_x = [
        pltpu.make_async_copy(guess.at[:, d, 0, :], xin.at[d], local_sem.at[d]) for d in range(DIRS)
    ]
    fetch_tables = [
        pltpu.make_async_copy(syn_hbm.at[me], syn.at[0], local_sem.at[3]),
        pltpu.make_async_copy(ana_hbm.at[me], ana.at[0], local_sem.at[4]),
        pltpu.make_async_copy(syn_hbm.at[twin], syn.at[1], local_sem.at[7 + DIRS]),
        pltpu.make_async_copy(ana_hbm.at[twin], ana.at[1], local_sem.at[8 + DIRS]),
    ]
    fetch_states = [
        pltpu.make_async_copy(states_hbm.at[:, peers[k], :], states.at[0, k], state_sem.at[k])
        for k in range(chips)
    ]
    fetch_tiles = [
        pltpu.make_async_copy(stiff_hbm.at[0, 0], stiff, local_sem.at[5]),
        pltpu.make_async_copy(mass_hbm.at[0, 0], mass, local_sem.at[6]),
    ]
    fetch_nodes = [
        pltpu.make_async_copy(preload_hbm, preload, node_sem.at[0]),
        pltpu.make_async_copy(normal_hbm, normal_stiff, node_sem.at[1]),
        pltpu.make_async_copy(tangent_hbm, tangent_stiff, node_sem.at[2]),
        pltpu.make_async_copy(friction_hbm, friction, node_sem.at[3]),
    ]
    fetch_links = pltpu.make_async_copy(links_hbm, links, node_sem.at[4])
    fetch_loads = [
        pltpu.make_async_copy(loads.at[:, d, 0, :], lin.at[d], local_sem.at[7 + d])
        for d in range(DIRS)
    ]
    fetch_links.start()
    for copy in fetch_x + fetch_nodes + fetch_tables + fetch_states[:1] + fetch_tiles + fetch_states[1:] + fetch_loads:
        copy.start()

    barrier = pltpu.get_barrier_semaphore()
    for peer in peers[1:] + [twin]:
        pl.semaphore_signal(barrier, inc=1, device_id=(peer, zone), device_id_type=MESH)
    for other in (before, after):
        pl.semaphore_signal(barrier, inc=1, device_id=(me, other), device_id_type=MESH)

    field[...] = jnp.zeros_like(field)
    load_field[...] = jnp.zeros_like(load_field)
    for copy in fetch_x:
        copy.wait()
    for d in range(DIRS):
        field[:coeff_count, d * BLOCK : (d + 1) * BLOCK] = xin[d]
    pl.semaphore_wait(barrier, chips + 2)

    row_id = lax.broadcasted_iota(jnp.int32, (ROWS, WIDTH), 0)
    order = ((row_id + 1) // 2).astype(jnp.float32)
    inertia = OMEGA_SQUARED * order * order
    constant_row = (lax.broadcasted_iota(jnp.int32, (ROWS, BLOCK), 0) == 0).astype(jnp.float32)

    def partial_forces(x, k, half):
        b = pl.ds(peers[k], 1)
        normal_x = x[:, :BLOCK] * normal_stiff[b, :] + constant_row * preload[b, :]
        high, low = split(jnp.concatenate([normal_x, x[:, BLOCK:]], axis=1))
        motion = mm(syn[half], jnp.concatenate([high, low, high], axis=0))
        state = states[half, k]
        u1 = motion[:, BLOCK : 2 * BLOCK]
        u2 = motion[:, 2 * BLOCK :]
        inverse = lax.rsqrt(u1 * u1 + u2 * u2 + SMOOTHING * SMOOTHING)
        normal = jnp.where(state > 0, motion[:, :BLOCK], 0.0)
        factor = jnp.where(state == 1, tangent_stiff[b, :], friction[b, :] * normal * inverse)
        f_high, f_low = split(jnp.concatenate([normal, factor * u1, factor * u2], axis=1))
        first = mm(ana[half], f_high)
        return first[:ROWS] + first[ROWS:] + mm(ana[half, :ROWS, :], f_low)

    def both(x):
        return jnp.concatenate(split(x), axis=0)

    def to_twin(ref, index, it, k):
        copy = pltpu.make_async_remote_copy(
            src_ref=ref.at[index],
            dst_ref=ref.at[index],
            send_sem=fwd_send.at[it, k],
            recv_sem=fwd_recv.at[it, k],
            device_id=(twin, zone),
            device_id_type=MESH,
        )
        copy.start()
        return copy

    sent = []
    residual = None
    pivots = None
    far_first = list(range(chips - 1, 0, -1))
    fetch_twin = []
    for it in range(ITERS):
        x = field[...]
        zone_x = (zone_first, zone_second)[it]
        zone_x[me] = x
        gather = {}
        for k in far_first:
            gather[k] = pltpu.make_async_remote_copy(
                src_ref=zone_x.at[me],
                dst_ref=zone_x.at[me],
                send_sem=ag_send.at[it, k],
                recv_sem=ag_recv.at[it, k],
                device_id=(peers[k], zone),
                device_id_type=MESH,
            )
            gather[k].start()
        forward = [to_twin(zone_x, me, it, 0)]
        near = []
        for side, other in enumerate((after, before)):
            copy = pltpu.make_async_remote_copy(
                src_ref=zone_x.at[me],
                dst_ref=near_x.at[it, side],
                send_sem=near_send.at[it, side],
                recv_sem=near_recv.at[it, side],
                device_id=(me, other),
                device_id_type=MESH,
            )
            copy.start()
            near.append(copy)
        if it == 0:
            for k in range(chips):
                copy = pltpu.make_async_remote_copy(
                    src_ref=states_hbm.at[:, twins[k], :],
                    dst_ref=states.at[1, k],
                    send_sem=st_send.at[k],
                    recv_sem=st_recv.at[k],
                    device_id=(twin, zone),
                    device_id_type=MESH,
                )
                copy.start()
                fetch_twin.append(copy)
            for copy in fetch_tables + fetch_nodes:
                copy.wait()
            fetch_states[0].wait()
        total = partial_forces(x, 0, 0)
        if it == 0:
            fetch_twin[0].wait_recv()
        total = total + partial_forces(x, 0, 1)
        if it == 0:
            for copy in fetch_tiles + fetch_loads:
                copy.wait()
            for d in range(DIRS):
                load_field[:coeff_count, d * BLOCK : (d + 1) * BLOCK] = lin[d]
            eye = lax.broadcasted_iota(jnp.int32, (BLOCK, BLOCK), 0) == lax.broadcasted_iota(
                jnp.int32, (BLOCK, BLOCK), 1
            )

            def diagonal(load):
                return jnp.concatenate(
                    [
                        jnp.sum(
                            jnp.where(eye, load(d).astype(jnp.float32), 0.0),
                            axis=0,
                            keepdims=True,
                        )
                        for d in range(DIRS)
                    ],
                    axis=1,
                )

            def tile(d):
                return pl.ds(d * BLOCK, BLOCK)

            pivots = diagonal(lambda d: stiff[0, tile(d), tile(d)]) - inertia * diagonal(
                lambda d: mass[tile(d), tile(d)]
            )
        coupled = mm(both(x), stiff[0]) + mm(both(-inertia * x), mass[...])
        scatter = []
        for k in range(1, chips):
            gather[k].wait_recv()
            forward.append(to_twin(zone_x, peers[k], it, k))
            if it == 0:
                fetch_states[k].wait()
                fetch_twin[k].wait_recv()
            arrived = zone_x[peers[k]]
            part[it, k] = partial_forces(arrived, k, 0) + partial_forces(arrived, k, 1)
            copy = pltpu.make_async_remote_copy(
                src_ref=part.at[it, k],
                dst_ref=recv.at[it, k],
                send_sem=rs_send.at[it, k],
                recv_sem=rs_recv.at[it, k],
                device_id=(peers[k], zone),
                device_id_type=MESH,
            )
            copy.start()
            scatter.append(copy)
        for side in range(2):
            near[side].wait_recv()
            coupled = coupled + mm(both(near_x[it, side]), stiff[1 + side])
        for copy in forward:
            copy.wait_recv()
        if it == 0:
            fetch_links.wait()
        for slot in range(3, 5):
            coupled = coupled + mm(both(zone_x[links[0, 0, slot - 3]]), stiff[slot])
        total = total + coupled[:ROWS] + coupled[ROWS:] - load_field[...]
        for k, copy in enumerate(scatter):
            copy.wait_recv()
            total = total + recv[it, k + 1]
        residual = total
        field[...] = x - residual / pivots
        sent += list(gather.values()) + near + scatter + forward

    stores = []
    for d in range(DIRS):
        lanes = pl.ds(d * BLOCK, BLOCK)
        xin[d] = field[:coeff_count, lanes]
        lin[d] = residual[:coeff_count, d * BLOCK : (d + 1) * BLOCK]
        stores.append(
            pltpu.make_async_copy(xin.at[d], out_coeff.at[:, d, 0, :], local_sem.at[d])
        )
        stores.append(
            pltpu.make_async_copy(lin.at[d], out_res.at[:, d, 0, :], local_sem.at[7 + d])
        )
    for copy in stores:
        copy.start()
    for copy in sent + fetch_twin:
        copy.wait_send()
    for copy in stores:
        copy.wait()


def solution(mesh):
    n = mesh.shape["tm"]
    zones = mesh.shape["zone"]

    def per_device(
        initial_guess,
        harmonic_loads,
        stiffness,
        mass_tiles,
        block_links,
        states,
        preload,
        normal_stiff,
        tangent_stiff,
        friction,
    ):
        coeff_count = initial_guess.shape[0]
        samples = states.shape[0]
        slots = stiffness.shape[2]
        syn, ana = trig_tables(samples * n, coeff_count, n)
        hbm = pl.BlockSpec(memory_space=pltpu.HBM)
        f32, bf16 = jnp.float32, jnp.bfloat16
        dma = pltpu.SemaphoreType.DMA
        out = jax.ShapeDtypeStruct(initial_guess.shape, f32)
        flat = [a.reshape(n, BLOCK) for a in (preload, normal_stiff, tangent_stiff, friction)]
        return pl.pallas_call(
            functools.partial(kernel, n, zones, coeff_count),
            out_shape=(out, out),
            in_specs=[hbm] * 12,
            out_specs=(hbm, hbm),
            scratch_shapes=[
                pltpu.VMEM((DIRS, coeff_count, BLOCK), f32),
                pltpu.VMEM((DIRS, coeff_count, BLOCK), f32),
                pltpu.VMEM((slots, WIDTH, WIDTH), bf16),
                pltpu.VMEM((WIDTH, WIDTH), bf16),
                pltpu.VMEM((2, n // 2, samples, BLOCK), jnp.int32),
                pltpu.VMEM((2, samples, 3 * ROWS), bf16),
                pltpu.VMEM((2, 2 * ROWS, samples), bf16),
                pltpu.VMEM((ROWS, WIDTH), f32),
                pltpu.VMEM((ROWS, WIDTH), f32),
                pltpu.VMEM((n, ROWS, WIDTH), f32),
                pltpu.VMEM((n, ROWS, WIDTH), f32),
                pltpu.VMEM((ITERS, 2, ROWS, WIDTH), f32),
                pltpu.VMEM((ITERS, n // 2, ROWS, WIDTH), f32),
                pltpu.VMEM((ITERS, n // 2, ROWS, WIDTH), f32),
                dma((9 + DIRS,)),
                dma((n // 2,)),
                dma((ITERS, n // 2)),
                dma((ITERS, n // 2)),
                dma((ITERS, 2)),
                dma((ITERS, 2)),
                dma((ITERS, n // 2)),
                dma((ITERS, n // 2)),
                dma((ITERS, n // 2)),
                dma((ITERS, n // 2)),
                dma((n // 2,)),
                dma((n // 2,)),
                dma((5,)),
                pltpu.SMEM((1, 1, 2), jnp.int32),
                pltpu.VMEM((n, BLOCK), f32),
                pltpu.VMEM((n, BLOCK), f32),
                pltpu.VMEM((n, BLOCK), f32),
                pltpu.VMEM((n, BLOCK), f32),
            ],
            compiler_params=pltpu.CompilerParams(
                collective_id=0, has_side_effects=True, vmem_limit_bytes=40 * 1024 * 1024
            ),
        )(
            *[
                pltpu.with_memory_space_constraint(operand, pltpu.HBM)
                for operand in (
                    initial_guess,
                    harmonic_loads,
                    stiffness,
                    mass_tiles,
                    block_links,
                    states.reshape(samples, n, BLOCK),
                    *flat,
                    jnp.asarray(syn),
                    jnp.asarray(ana),
                )
            ]
        )

    return jax.shard_map(
        per_device,
        mesh=mesh,
        in_specs=(
            P(None, None, "zone", "tm"),
            P(None, None, "zone", "tm"),
            P("zone", "tm", None, None, None),
            P("zone", "tm", None, None),
            P("zone", "tm", None),
            P("tm", "zone", None),
            P("zone", None),
            P("zone", None),
            P("zone", None),
            P("zone", None),
        ),
        out_specs=(P(None, None, "zone", "tm"), P(None, None, "zone", "tm")),
        check_vma=False,
    )
```

```python
import functools
import math

import jax
import jax.numpy as jnp
import ml_dtypes
import numpy as np
from jax import lax
from jax.experimental import pallas as pl
from jax.experimental.pallas import tpu as pltpu
from jax.sharding import PartitionSpec as P

DIRS = 3
BLOCK = 128
ITERS = 2
ROWS = 16
WIDTH = DIRS * BLOCK
OMEGA_SQUARED = 0.05
SMOOTHING = 0.1
MESH = pl.DeviceIdType.MESH


def split_np(table):
    high = table.astype(ml_dtypes.bfloat16)
    low = (table - high.astype(np.float64)).astype(ml_dtypes.bfloat16)
    return high, low


def trig_tables(total_samples, coeff_count, parts):
    rows = np.arange(coeff_count)
    orders = (rows + 1) // 2
    phases = (np.arange(total_samples)[:, None] * orders[None, :]) % total_samples
    angles = phases * (2.0 * math.pi / total_samples)
    is_sine = (rows % 2 == 0) & (rows > 0)
    synthesis = np.zeros((total_samples, ROWS))
    synthesis[:, :coeff_count] = np.where(is_sine[None, :], np.sin(angles), np.cos(angles))
    scaling = np.zeros(ROWS)
    scaling[:coeff_count] = np.where(orders == 0, 1.0, 2.0) / total_samples
    analysis = synthesis * scaling[None, :]
    s_high, s_low = split_np(synthesis)
    a_high, a_low = split_np(analysis)
    samples = total_samples // parts
    stacked = np.concatenate([s_high, s_high, s_low], axis=1).reshape(parts, samples, 3 * ROWS)
    stacked_t = np.concatenate([a_high, a_low], axis=1).reshape(parts, samples, 2 * ROWS)
    return stacked, np.ascontiguousarray(stacked_t.transpose(0, 2, 1))


def split(values):
    high = values.astype(jnp.bfloat16)
    low = (values - high.astype(jnp.float32)).astype(jnp.bfloat16)
    return high, low


def mm(a, b):
    return jnp.dot(a, b, preferred_element_type=jnp.float32)


def xor_index(index, k):
    result = index
    bit = 1
    while bit <= k:
        if k & bit:
            result = result + bit * (1 - 2 * ((index // bit) % 2))
        bit *= 2
    return result


def kernel(
    n,
    zones,
    coeff_count,
    guess,
    loads,
    stiff_hbm,
    mass_hbm,
    links_hbm,
    states_hbm,
    preload_hbm,
    normal_hbm,
    tangent_hbm,
    friction_hbm,
    syn_hbm,
    ana_hbm,
    out_coeff,
    out_res,
    xin,
    lin,
    stiff,
    mass,
    states,
    syn,
    ana,
    field,
    load_field,
    zone_first,
    zone_second,
    near_x,
    part,
    recv,
    local_sem,
    state_sem,
    ag_send,
    ag_recv,
    near_send,
    near_recv,
    rs_send,
    rs_recv,
    fwd_send,
    fwd_recv,
    st_send,
    st_recv,
    node_sem,
    links,
    preload,
    normal_stiff,
    tangent_stiff,
    friction,
):
    me = lax.axis_index("tm")
    zone = lax.axis_index("zone")
    before = lax.rem(zone + zones - 1, zones)
    after = lax.rem(zone + 1, zones)
    chips = n // 2
    chip = me // 2
    core = me % 2
    twin = me + 1 - 2 * core
    peers = [2 * xor_index(chip, k) + core for k in range(chips)]
    twins = [2 * xor_index(chip, k) + 1 - core for k in range(chips)]

    fetch_x = [
        pltpu.make_async_copy(guess.at[:, d, 0, :], xin.at[d], local_sem.at[d]) for d in range(DIRS)
    ]
    fetch_tables = [
        pltpu.make_async_copy(syn_hbm.at[me], syn.at[0], local_sem.at[3]),
        pltpu.make_async_copy(ana_hbm.at[me], ana.at[0], local_sem.at[4]),
        pltpu.make_async_copy(syn_hbm.at[twin], syn.at[1], local_sem.at[7 + DIRS]),
        pltpu.make_async_copy(ana_hbm.at[twin], ana.at[1], local_sem.at[8 + DIRS]),
    ]
    fetch_states = [
        pltpu.make_async_copy(states_hbm.at[:, peers[k], :], states.at[0, k], state_sem.at[k])
        for k in range(chips)
    ]
    fetch_tiles = [
        pltpu.make_async_copy(stiff_hbm.at[0, 0], stiff, local_sem.at[5]),
        pltpu.make_async_copy(mass_hbm.at[0, 0], mass, local_sem.at[6]),
    ]
    fetch_nodes = [
        pltpu.make_async_copy(preload_hbm, preload, node_sem.at[0]),
        pltpu.make_async_copy(normal_hbm, normal_stiff, node_sem.at[1]),
        pltpu.make_async_copy(tangent_hbm, tangent_stiff, node_sem.at[2]),
        pltpu.make_async_copy(friction_hbm, friction, node_sem.at[3]),
    ]
    fetch_links = pltpu.make_async_copy(links_hbm, links, node_sem.at[4])
    fetch_loads = [
        pltpu.make_async_copy(loads.at[:, d, 0, :], lin.at[d], local_sem.at[7 + d])
        for d in range(DIRS)
    ]
    fetch_links.start()
    for copy in fetch_x + fetch_nodes + fetch_tables + fetch_states[:1] + fetch_tiles + fetch_states[1:] + fetch_loads:
        copy.start()

    barrier = pltpu.get_barrier_semaphore()
    for peer in peers[1:] + [twin]:
        pl.semaphore_signal(barrier, inc=1, device_id=(peer, zone), device_id_type=MESH)
    for other in (before, after):
        pl.semaphore_signal(barrier, inc=1, device_id=(me, other), device_id_type=MESH)

    field[...] = jnp.zeros_like(field)
    load_field[...] = jnp.zeros_like(load_field)
    for copy in fetch_x:
        copy.wait()
    for d in range(DIRS):
        field[:coeff_count, d * BLOCK : (d + 1) * BLOCK] = xin[d]
    pl.semaphore_wait(barrier, chips + 2)

    row_id = lax.broadcasted_iota(jnp.int32, (ROWS, WIDTH), 0)
    order = ((row_id + 1) // 2).astype(jnp.float32)
    inertia = OMEGA_SQUARED * order * order
    constant_row = (lax.broadcasted_iota(jnp.int32, (ROWS, BLOCK), 0) == 0).astype(jnp.float32)

    def partial_forces(x, k, half):
        b = pl.ds(peers[k], 1)
        normal_x = x[:, :BLOCK] * normal_stiff[b, :] + constant_row * preload[b, :]
        high, low = split(jnp.concatenate([normal_x, x[:, BLOCK:]], axis=1))
        motion = mm(syn[half], jnp.concatenate([high, low, high], axis=0))
        state = states[half, k]
        u1 = motion[:, BLOCK : 2 * BLOCK]
        u2 = motion[:, 2 * BLOCK :]
        inverse = lax.rsqrt(u1 * u1 + u2 * u2 + SMOOTHING * SMOOTHING)
        normal = jnp.where(state > 0, motion[:, :BLOCK], 0.0)
        factor = jnp.where(state == 1, tangent_stiff[b, :], friction[b, :] * normal * inverse)
        f_high, f_low = split(jnp.concatenate([normal, factor * u1, factor * u2], axis=1))
        first = mm(ana[half], f_high)
        return first[:ROWS] + first[ROWS:] + mm(ana[half, :ROWS, :], f_low)

    def both(x):
        return jnp.concatenate(split(x), axis=0)

    def to_twin(ref, index, it, k):
        copy = pltpu.make_async_remote_copy(
            src_ref=ref.at[index],
            dst_ref=ref.at[index],
            send_sem=fwd_send.at[it, k],
            recv_sem=fwd_recv.at[it, k],
            device_id=(twin, zone),
            device_id_type=MESH,
        )
        copy.start()
        return copy

    sent = []
    residual = None
    pivots = None
    far_first = list(range(chips - 1, 0, -1))
    fetch_twin = []
    for it in range(ITERS):
        x = field[...]
        zone_x = (zone_first, zone_second)[it]
        zone_x[me] = x
        gather = {}
        for k in far_first:
            gather[k] = pltpu.make_async_remote_copy(
                src_ref=zone_x.at[me],
                dst_ref=zone_x.at[me],
                send_sem=ag_send.at[it, k],
                recv_sem=ag_recv.at[it, k],
                device_id=(peers[k], zone),
                device_id_type=MESH,
            )
            gather[k].start()
        forward = [to_twin(zone_x, me, it, 0)]
        near = []
        for side, other in enumerate((after, before)):
            copy = pltpu.make_async_remote_copy(
                src_ref=zone_x.at[me],
                dst_ref=near_x.at[it, side],
                send_sem=near_send.at[it, side],
                recv_sem=near_recv.at[it, side],
                device_id=(me, other),
                device_id_type=MESH,
            )
            copy.start()
            near.append(copy)
        if it == 0:
            for k in range(chips):
                copy = pltpu.make_async_remote_copy(
                    src_ref=states_hbm.at[:, twins[k], :],
                    dst_ref=states.at[1, k],
                    send_sem=st_send.at[k],
                    recv_sem=st_recv.at[k],
                    device_id=(twin, zone),
                    device_id_type=MESH,
                )
                copy.start()
                fetch_twin.append(copy)
            for copy in fetch_tables + fetch_nodes:
                copy.wait()
            fetch_states[0].wait()
        total = partial_forces(x, 0, 0)
        if it == 0:
            fetch_twin[0].wait_recv()
        total = total + partial_forces(x, 0, 1)
        if it == 0:
            for copy in fetch_tiles + fetch_loads:
                copy.wait()
            for d in range(DIRS):
                load_field[:coeff_count, d * BLOCK : (d + 1) * BLOCK] = lin[d]
            eye = lax.broadcasted_iota(jnp.int32, (BLOCK, BLOCK), 0) == lax.broadcasted_iota(
                jnp.int32, (BLOCK, BLOCK), 1
            )

            def diagonal(load):
                return jnp.concatenate(
                    [
                        jnp.sum(
                            jnp.where(eye, load(d).astype(jnp.float32), 0.0),
                            axis=0,
                            keepdims=True,
                        )
                        for d in range(DIRS)
                    ],
                    axis=1,
                )

            def tile(d):
                return pl.ds(d * BLOCK, BLOCK)

            pivots = diagonal(lambda d: stiff[0, tile(d), tile(d)]) - inertia * diagonal(
                lambda d: mass[tile(d), tile(d)]
            )
        coupled = mm(both(x), stiff[0]) + mm(both(-inertia * x), mass[...])
        scatter = []
        for k in range(1, chips):
            gather[k].wait_recv()
            forward.append(to_twin(zone_x, peers[k], it, k))
            if it == 0:
                fetch_states[k].wait()
                fetch_twin[k].wait_recv()
            arrived = zone_x[peers[k]]
            part[it, k] = partial_forces(arrived, k, 0) + partial_forces(arrived, k, 1)
            copy = pltpu.make_async_remote_copy(
                src_ref=part.at[it, k],
                dst_ref=recv.at[it, k],
                send_sem=rs_send.at[it, k],
                recv_sem=rs_recv.at[it, k],
                device_id=(peers[k], zone),
                device_id_type=MESH,
            )
            copy.start()
            scatter.append(copy)
        for side in range(2):
            near[side].wait_recv()
            coupled = coupled + mm(both(near_x[it, side]), stiff[1 + side])
        for copy in forward:
            copy.wait_recv()
        if it == 0:
            fetch_links.wait()
        for slot in range(3, 5):
            coupled = coupled + mm(both(zone_x[links[0, 0, slot - 3]]), stiff[slot])
        total = total + coupled[:ROWS] + coupled[ROWS:] - load_field[...]
        for k, copy in enumerate(scatter):
            copy.wait_recv()
            total = total + recv[it, k + 1]
        residual = total
        field[...] = x - residual / pivots
        sent += list(gather.values()) + near + scatter + forward

    for d in range(DIRS):
        lanes = pl.ds(d * BLOCK, BLOCK)
        out_coeff[:, d, 0, :] = field[:coeff_count, lanes]
        out_res[:, d, 0, :] = residual[:coeff_count, d * BLOCK : (d + 1) * BLOCK]
    for copy in sent + fetch_twin:
        copy.wait_send()


def solution(mesh):
    n = mesh.shape["tm"]
    zones = mesh.shape["zone"]

    def per_device(
        initial_guess,
        harmonic_loads,
        stiffness,
        mass_tiles,
        block_links,
        states,
        preload,
        normal_stiff,
        tangent_stiff,
        friction,
    ):
        coeff_count = initial_guess.shape[0]
        samples = states.shape[0]
        slots = stiffness.shape[2]
        syn, ana = trig_tables(samples * n, coeff_count, n)
        hbm = pl.BlockSpec(memory_space=pltpu.HBM)
        f32, bf16 = jnp.float32, jnp.bfloat16
        dma = pltpu.SemaphoreType.DMA
        out = jax.ShapeDtypeStruct(initial_guess.shape, f32)
        flat = [a.reshape(n, BLOCK) for a in (preload, normal_stiff, tangent_stiff, friction)]
        return pl.pallas_call(
            functools.partial(kernel, n, zones, coeff_count),
            out_shape=(out, out),
            in_specs=[hbm] * 12,
            out_specs=(pl.BlockSpec(memory_space=pltpu.VMEM),) * 2,
            scratch_shapes=[
                pltpu.VMEM((DIRS, coeff_count, BLOCK), f32),
                pltpu.VMEM((DIRS, coeff_count, BLOCK), f32),
                pltpu.VMEM((slots, WIDTH, WIDTH), bf16),
                pltpu.VMEM((WIDTH, WIDTH), bf16),
                pltpu.VMEM((2, n // 2, samples, BLOCK), jnp.int32),
                pltpu.VMEM((2, samples, 3 * ROWS), bf16),
                pltpu.VMEM((2, 2 * ROWS, samples), bf16),
                pltpu.VMEM((ROWS, WIDTH), f32),
                pltpu.VMEM((ROWS, WIDTH), f32),
                pltpu.VMEM((n, ROWS, WIDTH), f32),
                pltpu.VMEM((n, ROWS, WIDTH), f32),
                pltpu.VMEM((ITERS, 2, ROWS, WIDTH), f32),
                pltpu.VMEM((ITERS, n // 2, ROWS, WIDTH), f32),
                pltpu.VMEM((ITERS, n // 2, ROWS, WIDTH), f32),
                dma((9 + DIRS,)),
                dma((n // 2,)),
                dma((ITERS, n // 2)),
                dma((ITERS, n // 2)),
                dma((ITERS, 2)),
                dma((ITERS, 2)),
                dma((ITERS, n // 2)),
                dma((ITERS, n // 2)),
                dma((ITERS, n // 2)),
                dma((ITERS, n // 2)),
                dma((n // 2,)),
                dma((n // 2,)),
                dma((5,)),
                pltpu.SMEM((1, 1, 2), jnp.int32),
                pltpu.VMEM((n, BLOCK), f32),
                pltpu.VMEM((n, BLOCK), f32),
                pltpu.VMEM((n, BLOCK), f32),
                pltpu.VMEM((n, BLOCK), f32),
            ],
            compiler_params=pltpu.CompilerParams(
                collective_id=0, has_side_effects=True, vmem_limit_bytes=40 * 1024 * 1024
            ),
        )(
            *[
                pltpu.with_memory_space_constraint(operand, pltpu.HBM)
                for operand in (
                    initial_guess,
                    harmonic_loads,
                    stiffness,
                    mass_tiles,
                    block_links,
                    states.reshape(samples, n, BLOCK),
                    *flat,
                    jnp.asarray(syn),
                    jnp.asarray(ana),
                )
            ]
        )

    return jax.shard_map(
        per_device,
        mesh=mesh,
        in_specs=(
            P(None, None, "zone", "tm"),
            P(None, None, "zone", "tm"),
            P("zone", "tm", None, None, None),
            P("zone", "tm", None, None),
            P("zone", "tm", None),
            P("tm", "zone", None),
            P("zone", None),
            P("zone", None),
            P("zone", None),
            P("zone", None),
        ),
        out_specs=(P(None, None, "zone", "tm"), P(None, None, "zone", "tm")),
        check_vma=False,
    )
```

```python
import functools
import math

import jax
import jax.numpy as jnp
import ml_dtypes
import numpy as np
from jax import lax
from jax.experimental import pallas as pl
from jax.experimental.pallas import tpu as pltpu
from jax.sharding import PartitionSpec as P

DIRS = 3
BLOCK = 128
ITERS = 2
ROWS = 16
WIDTH = DIRS * BLOCK
OMEGA_SQUARED = 0.05
SMOOTHING = 0.1
MESH = pl.DeviceIdType.MESH


def split_np(table):
    high = table.astype(ml_dtypes.bfloat16)
    low = (table - high.astype(np.float64)).astype(ml_dtypes.bfloat16)
    return high, low


def trig_tables(total_samples, coeff_count, parts):
    rows = np.arange(coeff_count)
    orders = (rows + 1) // 2
    phases = (np.arange(total_samples)[:, None] * orders[None, :]) % total_samples
    angles = phases * (2.0 * math.pi / total_samples)
    is_sine = (rows % 2 == 0) & (rows > 0)
    synthesis = np.zeros((total_samples, ROWS))
    synthesis[:, :coeff_count] = np.where(is_sine[None, :], np.sin(angles), np.cos(angles))
    scaling = np.zeros(ROWS)
    scaling[:coeff_count] = np.where(orders == 0, 1.0, 2.0) / total_samples
    analysis = synthesis * scaling[None, :]
    s_high, s_low = split_np(synthesis)
    a_high, a_low = split_np(analysis)
    samples = total_samples // parts
    stacked = np.concatenate([s_high, s_high, s_low], axis=1).reshape(parts, samples, 3 * ROWS)
    stacked_t = np.concatenate([a_high, a_low], axis=1).reshape(parts, samples, 2 * ROWS)
    return stacked, np.ascontiguousarray(stacked_t.transpose(0, 2, 1))


def split(values):
    high = values.astype(jnp.bfloat16)
    low = (values - high.astype(jnp.float32)).astype(jnp.bfloat16)
    return high, low


def mm(a, b):
    return jnp.dot(a, b, preferred_element_type=jnp.float32)


def xor_index(index, k):
    result = index
    bit = 1
    while bit <= k:
        if k & bit:
            result = result + bit * (1 - 2 * ((index // bit) % 2))
        bit *= 2
    return result


def kernel(
    n,
    zones,
    coeff_count,
    guess,
    loads,
    stiff_hbm,
    mass_hbm,
    links_hbm,
    states_hbm,
    preload_hbm,
    normal_hbm,
    tangent_hbm,
    friction_hbm,
    syn_hbm,
    ana_hbm,
    out_coeff,
    out_res,
    xin,
    lin,
    stiff,
    mass,
    states,
    syn,
    ana,
    field,
    load_field,
    zone_first,
    zone_second,
    near_x,
    part,
    recv,
    local_sem,
    state_sem,
    ag_send,
    ag_recv,
    near_send,
    near_recv,
    rs_send,
    rs_recv,
    fwd_send,
    fwd_recv,
    st_send,
    st_recv,
    node_sem,
    links,
    preload,
    normal_stiff,
    tangent_stiff,
    friction,
):
    me = lax.axis_index("tm")
    zone = lax.axis_index("zone")
    before = lax.rem(zone + zones - 1, zones)
    after = lax.rem(zone + 1, zones)
    chips = n // 2
    chip = me // 2
    core = me % 2
    twin = me + 1 - 2 * core
    peers = [2 * xor_index(chip, k) + core for k in range(chips)]
    twins = [2 * xor_index(chip, k) + 1 - core for k in range(chips)]

    fetch_x = [
        pltpu.make_async_copy(guess.at[:, d, 0, :], xin.at[d], local_sem.at[d]) for d in range(DIRS)
    ]
    fetch_tables = [
        pltpu.make_async_copy(syn_hbm.at[me], syn.at[0], local_sem.at[3]),
        pltpu.make_async_copy(ana_hbm.at[me], ana.at[0], local_sem.at[4]),
        pltpu.make_async_copy(syn_hbm.at[twin], syn.at[1], local_sem.at[7 + DIRS]),
        pltpu.make_async_copy(ana_hbm.at[twin], ana.at[1], local_sem.at[8 + DIRS]),
    ]
    fetch_states = [
        pltpu.make_async_copy(states_hbm.at[:, peers[k], :], states.at[0, k], state_sem.at[k])
        for k in range(chips)
    ]
    fetch_tiles = [
        pltpu.make_async_copy(stiff_hbm.at[0, 0], stiff, local_sem.at[5]),
        pltpu.make_async_copy(mass_hbm.at[0, 0], mass, local_sem.at[6]),
    ]
    fetch_nodes = [
        pltpu.make_async_copy(preload_hbm, preload, node_sem.at[0]),
        pltpu.make_async_copy(normal_hbm, normal_stiff, node_sem.at[1]),
        pltpu.make_async_copy(tangent_hbm, tangent_stiff, node_sem.at[2]),
        pltpu.make_async_copy(friction_hbm, friction, node_sem.at[3]),
    ]
    fetch_links = pltpu.make_async_copy(links_hbm, links, node_sem.at[4])
    fetch_loads = [
        pltpu.make_async_copy(loads.at[:, d, 0, :], lin.at[d], local_sem.at[7 + d])
        for d in range(DIRS)
    ]
    fetch_links.start()
    for copy in fetch_x + fetch_nodes + fetch_tables + fetch_states[:1] + fetch_tiles + fetch_states[1:] + fetch_loads:
        copy.start()

    barrier = pltpu.get_barrier_semaphore()
    for peer in peers[1:] + [twin]:
        pl.semaphore_signal(barrier, inc=1, device_id=(peer, zone), device_id_type=MESH)
    for other in (before, after):
        pl.semaphore_signal(barrier, inc=1, device_id=(me, other), device_id_type=MESH)

    field[...] = jnp.zeros_like(field)
    load_field[...] = jnp.zeros_like(load_field)
    for copy in fetch_x:
        copy.wait()
    for d in range(DIRS):
        field[:coeff_count, d * BLOCK : (d + 1) * BLOCK] = xin[d]
    pl.semaphore_wait(barrier, chips + 2)

    row_id = lax.broadcasted_iota(jnp.int32, (ROWS, WIDTH), 0)
    order = ((row_id + 1) // 2).astype(jnp.float32)
    inertia = OMEGA_SQUARED * order * order
    constant_row = (lax.broadcasted_iota(jnp.int32, (ROWS, BLOCK), 0) == 0).astype(jnp.float32)

    def partial_forces(x, k, half):
        b = pl.ds(peers[k], 1)
        normal_x = x[:, :BLOCK] * normal_stiff[b, :] + constant_row * preload[b, :]
        high, low = split(jnp.concatenate([normal_x, x[:, BLOCK:]], axis=1))
        samples = syn.shape[1]
        count = len(half) * samples
        table = syn[half[0] : half[-1] + 1].reshape(count, 3 * ROWS)
        motion = mm(table, jnp.concatenate([high, low, high], axis=0))
        state = states[half[0] : half[-1] + 1, k].reshape(count, BLOCK)
        u1 = motion[:, BLOCK : 2 * BLOCK]
        u2 = motion[:, 2 * BLOCK :]
        inverse = lax.rsqrt(u1 * u1 + u2 * u2 + SMOOTHING * SMOOTHING)
        normal = jnp.where(state > 0, motion[:, :BLOCK], 0.0)
        factor = jnp.where(state == 1, tangent_stiff[b, :], friction[b, :] * normal * inverse)
        f_high, f_low = split(jnp.concatenate([normal, factor * u1, factor * u2], axis=1))
        result = None
        for i, h in enumerate(half):
            rows = slice(i * samples, (i + 1) * samples)
            first = mm(ana[h], f_high[rows])
            term = first[:ROWS] + first[ROWS:] + mm(ana[h, :ROWS, :], f_low[rows])
            result = term if result is None else result + term
        return result

    def both(x):
        return jnp.concatenate(split(x), axis=0)

    def to_twin(ref, index, it, k):
        copy = pltpu.make_async_remote_copy(
            src_ref=ref.at[index],
            dst_ref=ref.at[index],
            send_sem=fwd_send.at[it, k],
            recv_sem=fwd_recv.at[it, k],
            device_id=(twin, zone),
            device_id_type=MESH,
        )
        copy.start()
        return copy

    sent = []
    residual = None
    pivots = None
    far_first = list(range(chips - 1, 0, -1))
    fetch_twin = []
    for it in range(ITERS):
        x = field[...]
        zone_x = (zone_first, zone_second)[it]
        zone_x[me] = x
        gather = {}
        for k in far_first:
            gather[k] = pltpu.make_async_remote_copy(
                src_ref=zone_x.at[me],
                dst_ref=zone_x.at[me],
                send_sem=ag_send.at[it, k],
                recv_sem=ag_recv.at[it, k],
                device_id=(peers[k], zone),
                device_id_type=MESH,
            )
            gather[k].start()
        forward = [to_twin(zone_x, me, it, 0)]
        near = []
        for side, other in enumerate((after, before)):
            copy = pltpu.make_async_remote_copy(
                src_ref=zone_x.at[me],
                dst_ref=near_x.at[it, side],
                send_sem=near_send.at[it, side],
                recv_sem=near_recv.at[it, side],
                device_id=(me, other),
                device_id_type=MESH,
            )
            copy.start()
            near.append(copy)
        if it == 0:
            for k in range(chips):
                copy = pltpu.make_async_remote_copy(
                    src_ref=states_hbm.at[:, twins[k], :],
                    dst_ref=states.at[1, k],
                    send_sem=st_send.at[k],
                    recv_sem=st_recv.at[k],
                    device_id=(twin, zone),
                    device_id_type=MESH,
                )
                copy.start()
                fetch_twin.append(copy)
            for copy in fetch_tables + fetch_nodes:
                copy.wait()
            fetch_states[0].wait()
        if it == 0:
            total = partial_forces(x, 0, (0,))
            fetch_twin[0].wait_recv()
            total = total + partial_forces(x, 0, (1,))
        else:
            total = partial_forces(x, 0, (0, 1))
        if it == 0:
            for copy in fetch_tiles + fetch_loads:
                copy.wait()
            for d in range(DIRS):
                load_field[:coeff_count, d * BLOCK : (d + 1) * BLOCK] = lin[d]
            eye = lax.broadcasted_iota(jnp.int32, (BLOCK, BLOCK), 0) == lax.broadcasted_iota(
                jnp.int32, (BLOCK, BLOCK), 1
            )

            def diagonal(load):
                return jnp.concatenate(
                    [
                        jnp.sum(
                            jnp.where(eye, load(d).astype(jnp.float32), 0.0),
                            axis=0,
                            keepdims=True,
                        )
                        for d in range(DIRS)
                    ],
                    axis=1,
                )

            def tile(d):
                return pl.ds(d * BLOCK, BLOCK)

            pivots = diagonal(lambda d: stiff[0, tile(d), tile(d)]) - inertia * diagonal(
                lambda d: mass[tile(d), tile(d)]
            )
        coupled = mm(both(x), stiff[0]) + mm(both(-inertia * x), mass[...])
        scatter = []
        for k in range(1, chips):
            gather[k].wait_recv()
            forward.append(to_twin(zone_x, peers[k], it, k))
            if it == 0:
                fetch_states[k].wait()
                fetch_twin[k].wait_recv()
            arrived = zone_x[peers[k]]
            part[it, k] = partial_forces(arrived, k, (0, 1))
            copy = pltpu.make_async_remote_copy(
                src_ref=part.at[it, k],
                dst_ref=recv.at[it, k],
                send_sem=rs_send.at[it, k],
                recv_sem=rs_recv.at[it, k],
                device_id=(peers[k], zone),
                device_id_type=MESH,
            )
            copy.start()
            scatter.append(copy)
        for side in range(2):
            near[side].wait_recv()
            coupled = coupled + mm(both(near_x[it, side]), stiff[1 + side])
        for copy in forward:
            copy.wait_recv()
        if it == 0:
            fetch_links.wait()
        for slot in range(3, 5):
            coupled = coupled + mm(both(zone_x[links[0, 0, slot - 3]]), stiff[slot])
        total = total + coupled[:ROWS] + coupled[ROWS:] - load_field[...]
        for k, copy in enumerate(scatter):
            copy.wait_recv()
            total = total + recv[it, k + 1]
        residual = total
        field[...] = x - residual / pivots
        sent += list(gather.values()) + near + scatter + forward

    for d in range(DIRS):
        lanes = pl.ds(d * BLOCK, BLOCK)
        out_coeff[:, d, 0, :] = field[:coeff_count, lanes]
        out_res[:, d, 0, :] = residual[:coeff_count, d * BLOCK : (d + 1) * BLOCK]
    for copy in sent + fetch_twin:
        copy.wait_send()


def solution(mesh):
    n = mesh.shape["tm"]
    zones = mesh.shape["zone"]

    def per_device(
        initial_guess,
        harmonic_loads,
        stiffness,
        mass_tiles,
        block_links,
        states,
        preload,
        normal_stiff,
        tangent_stiff,
        friction,
    ):
        coeff_count = initial_guess.shape[0]
        samples = states.shape[0]
        slots = stiffness.shape[2]
        syn, ana = trig_tables(samples * n, coeff_count, n)
        hbm = pl.BlockSpec(memory_space=pltpu.HBM)
        f32, bf16 = jnp.float32, jnp.bfloat16
        dma = pltpu.SemaphoreType.DMA
        out = jax.ShapeDtypeStruct(initial_guess.shape, f32)
        flat = [a.reshape(n, BLOCK) for a in (preload, normal_stiff, tangent_stiff, friction)]
        return pl.pallas_call(
            functools.partial(kernel, n, zones, coeff_count),
            out_shape=(out, out),
            in_specs=[hbm] * 12,
            out_specs=(pl.BlockSpec(memory_space=pltpu.VMEM),) * 2,
            scratch_shapes=[
                pltpu.VMEM((DIRS, coeff_count, BLOCK), f32),
                pltpu.VMEM((DIRS, coeff_count, BLOCK), f32),
                pltpu.VMEM((slots, WIDTH, WIDTH), bf16),
                pltpu.VMEM((WIDTH, WIDTH), bf16),
                pltpu.VMEM((2, n // 2, samples, BLOCK), jnp.int32),
                pltpu.VMEM((2, samples, 3 * ROWS), bf16),
                pltpu.VMEM((2, 2 * ROWS, samples), bf16),
                pltpu.VMEM((ROWS, WIDTH), f32),
                pltpu.VMEM((ROWS, WIDTH), f32),
                pltpu.VMEM((n, ROWS, WIDTH), f32),
                pltpu.VMEM((n, ROWS, WIDTH), f32),
                pltpu.VMEM((ITERS, 2, ROWS, WIDTH), f32),
                pltpu.VMEM((ITERS, n // 2, ROWS, WIDTH), f32),
                pltpu.VMEM((ITERS, n // 2, ROWS, WIDTH), f32),
                dma((9 + DIRS,)),
                dma((n // 2,)),
                dma((ITERS, n // 2)),
                dma((ITERS, n // 2)),
                dma((ITERS, 2)),
                dma((ITERS, 2)),
                dma((ITERS, n // 2)),
                dma((ITERS, n // 2)),
                dma((ITERS, n // 2)),
                dma((ITERS, n // 2)),
                dma((n // 2,)),
                dma((n // 2,)),
                dma((5,)),
                pltpu.SMEM((1, 1, 2), jnp.int32),
                pltpu.VMEM((n, BLOCK), f32),
                pltpu.VMEM((n, BLOCK), f32),
                pltpu.VMEM((n, BLOCK), f32),
                pltpu.VMEM((n, BLOCK), f32),
            ],
            compiler_params=pltpu.CompilerParams(
                collective_id=0, has_side_effects=True, vmem_limit_bytes=40 * 1024 * 1024
            ),
        )(
            *[
                pltpu.with_memory_space_constraint(operand, pltpu.HBM)
                for operand in (
                    initial_guess,
                    harmonic_loads,
                    stiffness,
                    mass_tiles,
                    block_links,
                    states.reshape(samples, n, BLOCK),
                    *flat,
                    jnp.asarray(syn),
                    jnp.asarray(ana),
                )
            ]
        )

    return jax.shard_map(
        per_device,
        mesh=mesh,
        in_specs=(
            P(None, None, "zone", "tm"),
            P(None, None, "zone", "tm"),
            P("zone", "tm", None, None, None),
            P("zone", "tm", None, None),
            P("zone", "tm", None),
            P("tm", "zone", None),
            P("zone", None),
            P("zone", None),
            P("zone", None),
            P("zone", None),
        ),
        out_specs=(P(None, None, "zone", "tm"), P(None, None, "zone", "tm")),
        check_vma=False,
    )
```
